32 devices in a mesh: row: 8 (over y, x, core), col: 4 (over z).
Axes of the slice: x: 2, y: 2, z: 4, core: 2. Of those that a mesh axis runs over, the one named last changes fastest.
Arguments:
- replicas: bfloat16 [2560, 10240], P('row', 'col'), may hold values from -24 to 24
- factor_seeds: int32 [2, 2, 2, 2], replicated, may hold values from 0 to 8190
- edge_counts: int32 [2, 2, 2], replicated, may hold values from 1 to 4
Outputs:
- update: float32 [2560, 10240], P('row', 'col')
The draws below stay inside these ranges and needn't reach their ends.
All inputs are finite; a program needn't handle non-finite values.
Results may differ from the reference program's by a relative error of at most 0.0003.
Values sent between devices are 32-bit elements; how exact they have to be, the bound alone decides.
No kernel may reach another device: no remote copies, remote signals or barrier semaphores. Data moves between devices by JAX's collectives and lax.ppermute only.
A program may use at most 64 MiB of HBM per device.

```python
import jax
import jax.numpy as jnp
from jax import lax

D_MODEL = 1280
HIDDEN_SIZE = 5120
RANK = 2
ROUNDS = 2
GRAPH_ROWS = 2
GRAPH_COLS = 2


def touch_ends(entries, own_key, low, high):
    extent = entries.shape
    place = [jax.random.randint(jax.random.fold_in(own_key, axis), (), 0, extent[axis]) for axis in range(len(extent))]
    entries = entries.at[tuple(place)].set(low)
    longest = extent.index(max(extent))
    place[longest] = (place[longest] + 1) % extent[longest]
    return entries.at[tuple(place)].set(high)


def steps_of(rng, shape, shards, low, top_value):
    loudness = 1.0
    for dim, shards_of in shards:
        draws = jax.random.uniform(jax.random.fold_in(jax.random.fold_in(rng, 6), dim), (shards_of,), jnp.float32, low / len(shards), top_value / len(shards))
        loudness = loudness * jnp.repeat(jnp.exp(draws), shape[dim] // shards_of).reshape((-1,) + (1,) * (len(shape) - 1 - dim))
    return loudness


def centred(key, dims, width, limit, pieces=(), kind=jnp.bfloat16):
    entries = width * jax.random.normal(key, dims, jnp.float32)
    if pieces:
        entries = entries * steps_of(key, dims, pieces, -0.22, 0.18)
    return jnp.clip(entries, -limit, limit).astype(kind)


def setup_inputs(seed: int = 0) -> dict:
    key_of = jax.random.split(jax.random.key(seed), 4)
    return {
        "replicas": centred(key_of[0], (GRAPH_ROWS * D_MODEL, GRAPH_COLS * HIDDEN_SIZE), 4.0, 24.0, ((0, 8), (1, 4))),
        "factor_seeds": touch_ends(jax.random.randint(key_of[1], (GRAPH_ROWS, GRAPH_COLS, 2, RANK), 0, 8191), jax.random.fold_in(key_of[1], 1), 0, 8190).astype(jnp.int32),
        "edge_counts": touch_ends(jax.random.randint(key_of[2], (GRAPH_ROWS, GRAPH_COLS, 2), 1, 5), jax.random.fold_in(key_of[2], 1), 1, 4).astype(jnp.int32),
    }


highest = lax.Precision.HIGHEST
epsilon = 1e-06

def start_factors(factor_seeds):
    column = jnp.arange(HIDDEN_SIZE, dtype=jnp.int32)
    square = column * column % 8191
    residue = (square * (factor_seeds[..., None] + 1) + column * 17) % 8191
    return residue.astype(jnp.float32) * (2.0 / 8191.0) - 1.0

def images_of(replica_blocks, update_blocks, vectors):
    if update_blocks is None:

        def one_row(row_items):
            row_block, row_vectors = row_items
            return jnp.einsum('cjm,kcm->cjk', row_vectors, row_block.astype(jnp.float32), precision=highest)
        return lax.map(one_row, (replica_blocks, vectors))

    def one_row_more(row_items):
        row_block, row_update, row_vectors = row_items
        leading = jnp.einsum('cjm,kcm->cjk', row_vectors, row_block.astype(jnp.float32), precision=highest)
        return leading + jnp.einsum('cjm,kcm->cjk', row_vectors, row_update, precision=highest)
    return lax.map(one_row_more, (replica_blocks, update_blocks, vectors))

def projections_of(replica_blocks, update_blocks, directions):
    if update_blocks is None:

        def one_row(row_items):
            row_block, row_vectors = row_items
            return jnp.einsum('cjk,kcm->cjm', row_vectors, row_block.astype(jnp.float32), precision=highest)
        return lax.map(one_row, (replica_blocks, directions))

    def one_row_more(row_items):
        row_block, row_update, row_vectors = row_items
        leading = jnp.einsum('cjk,kcm->cjm', row_vectors, row_block.astype(jnp.float32), precision=highest)
        return leading + jnp.einsum('cjk,kcm->cjm', row_vectors, row_update, precision=highest)
    return lax.map(one_row_more, (replica_blocks, update_blocks, directions))

def orthonormal(values):
    leading = values[..., 0, :]
    second = values[..., 1, :]
    lead_norm = lax.optimization_barrier(jnp.sum(leading * leading, -1, keepdims=True))
    leading = leading / jnp.sqrt(lead_norm + epsilon)
    correlation = lax.optimization_barrier(jnp.sum(leading * second, -1, keepdims=True))
    second = second - correlation * leading
    rest_norm = lax.optimization_barrier(jnp.sum(second * second, -1, keepdims=True))
    second = second / jnp.sqrt(rest_norm + epsilon)
    return jnp.stack([leading, second], -2)

def reference(replicas, factor_seeds, edge_counts):
    replica_blocks = replicas.reshape(GRAPH_ROWS, D_MODEL, GRAPH_COLS, HIDDEN_SIZE)
    initial = start_factors(factor_seeds)
    factors = [initial[:, :, 0], initial[:, :, 1]]
    scales = [edge_counts[:, :, 0].astype(jnp.float32) / 16.0, edge_counts[:, :, 1].astype(jnp.float32) / 16.0]
    update_blocks = None
    for round_index in range(ROUNDS):
        left_factors = []
        right_factors = []
        fresh_list = []
        for graph_axis in range(2):
            vectors = factors[graph_axis]
            own_images = images_of(replica_blocks, update_blocks, vectors)
            other_images = jnp.roll(images_of(replica_blocks, update_blocks, jnp.roll(vectors, 1, graph_axis)), -1, graph_axis)
            directions = orthonormal(own_images - other_images)
            mine = projections_of(replica_blocks, update_blocks, directions)
            theirs = jnp.roll(projections_of(replica_blocks, update_blocks, jnp.roll(directions, 1, graph_axis)), -1, graph_axis)
            fresh_factors = mine - theirs
            fresh_list.append(fresh_factors)
            edge_scale = scales[graph_axis][:, :, None, None]
            left_factors += [directions, jnp.roll(directions, 1, graph_axis)]
            right_factors += [-edge_scale * fresh_factors, jnp.roll(edge_scale * fresh_factors, 1, graph_axis)]
        factors = fresh_list
        left_stack = jnp.stack(left_factors, 2)
        right_stack = jnp.stack(right_factors, 2)

        def one_row(row_items):
            return jnp.einsum('cejk,cejm->kcm', row_items[0], row_items[1], precision=highest)
        correction = lax.map(one_row, (left_stack, right_stack))
        update_blocks = correction if update_blocks is None else update_blocks + correction
    return update_blocks.reshape(GRAPH_ROWS * D_MODEL, GRAPH_COLS * HIDDEN_SIZE)
```

```python
import jax
import jax.numpy as jnp
from jax import lax
from jax.sharding import PartitionSpec as P

ROUNDS = 2
MODULUS_BITS = 13
MODULUS = (1 << MODULUS_BITS) - 1

highest = lax.Precision.HIGHEST
epsilon = 1e-06


def remainder(value):
    value = (value & MODULUS) + (value >> MODULUS_BITS)
    value = (value & MODULUS) + (value >> MODULUS_BITS)
    return jnp.where(value >= MODULUS, value - MODULUS, value)


def start_factors(seeds, first_column, width):
    column = first_column + jnp.arange(width, dtype=jnp.int32)
    square = remainder(column * column)
    residue = remainder(square * (seeds[:, None] + 1) + column * 17)
    return residue.astype(jnp.float32) * (2.0 / MODULUS) - 1.0


def two_terms(values):
    high = lax.reduce_precision(values, 8, 7)
    low = values - high
    return high.astype(jnp.bfloat16), low.astype(jnp.bfloat16)


def times_exact(values, exact, dimension):
    count = values.shape[0]
    terms = jnp.concatenate(two_terms(values), 0)
    product = lax.dot_general(
        terms, exact, (((1,), (dimension,)), ((), ())), preferred_element_type=jnp.float32
    )
    return product[:count] + product[count:]


def small_product(left, right, left_dim, right_dim):
    return lax.dot_general(
        left,
        right,
        (((left_dim,), (right_dim,)), ((), ())),
        precision=highest,
        preferred_element_type=jnp.float32,
    )


class Layout:
    def __init__(self, graph_rows, graph_cols):
        self.rows, self.cols = lax.axis_size("row"), lax.axis_size("col")
        self.nodes = (graph_rows, graph_cols)
        self.shards = (self.rows // graph_rows, self.cols // graph_cols)

    def exchange(self, value, target):
        pairs = []
        for r in range(self.rows):
            for c in range(self.cols):
                tr, tc = target(r, c)
                pairs.append((r * self.cols + c, tr * self.cols + tc))
        return lax.ppermute(value, ("row", "col"), pairs)

    def row_swap(self, value, bit):
        return self.exchange(value, lambda r, c: (r ^ 1 << bit, c))

    def col_swap(self, value, bit):
        return self.exchange(value, lambda r, c: (r, c ^ 1 << bit))

    def step(self, half, by):
        def target(r, c):
            if (r & 1) == half:
                return (r + by * self.shards[0]) % self.rows, c
            return r, (c + by * self.shards[1]) % self.cols

        return target

    def neighbours(self, value, half):
        if self.nodes == (2, 2):
            other = self.exchange(value, self.step(half, 1))
            return jnp.concatenate([other[2:], other[:2]], 0)
        after = self.exchange(value[2:], self.step(half, -1))
        before = self.exchange(value[:2], self.step(half, 1))
        return jnp.concatenate([after, before], 0)


def per_device(replicas, factor_seeds, edge_counts):
    local_rows, local_cols = replicas.shape
    graph_rows, graph_cols = factor_seeds.shape[:2]
    layout = Layout(graph_rows, graph_cols)
    row_index, col_index = lax.axis_index("row"), lax.axis_index("col")
    node_row, node_col = row_index // layout.shards[0], col_index // layout.shards[1]
    first_column = col_index % layout.shards[1] * local_cols
    above_row = (node_row + graph_rows - 1) % graph_rows
    left_col = (node_col + graph_cols - 1) % graph_cols
    first_half = row_index & 1
    edges = []
    for half in range(2):
        along_col = first_half ^ half
        edges.append((node_row, node_col, along_col))
        edges.append(
            (
                jnp.where(along_col == 0, above_row, node_row),
                jnp.where(along_col == 0, node_col, left_col),
                along_col,
            )
        )
    seeds = jnp.concatenate([factor_seeds[r, c, a] for r, c, a in edges])
    counts = jnp.stack([edge_counts[r, c, a] for r, c, a in edges])
    scaling = -(counts.astype(jnp.float32) / 16.0)

    factors = start_factors(seeds, first_column, local_cols)
    lefts, rights = [], []
    for round_index in range(ROUNDS):
        images = times_exact(factors, replicas, 1)
        for left, right in zip(lefts, rights):
            images = images + small_product(small_product(factors, right, 1, 1), left, 1, 0)
        for bit in range(layout.shards[1].bit_length() - 1):
            images = images + layout.col_swap(images, bit)
        others = [layout.neighbours(images[4 * half : 4 * half + 4], half) for half in range(2)]
        left = images - jnp.concatenate(others, 0)

        projections = times_exact(left, replicas, 0)
        for earlier, right in zip(lefts, rights):
            projections = projections + small_product(small_product(left, earlier, 1, 1), right, 1, 0)
        pairs = left.reshape(4, 2, local_rows)
        inner = jnp.sum(pairs[:, :, None] * pairs[:, None, :], -1).reshape(8, 2)
        packed = jnp.concatenate([projections, jnp.pad(inner, ((0, 0), (0, 126)))], 1)
        total = packed[:4] + layout.row_swap(packed[4:], 0)
        for bit in range(1, layout.shards[0].bit_length() - 1):
            total = total + layout.row_swap(total, bit)
        total = total + layout.neighbours(total, 0)
        total = jnp.concatenate([total, layout.row_swap(total, 0)], 0)

        raw = total[:, :local_cols].reshape(4, 2, local_cols)
        gram = 0.5 * total[:, local_cols : local_cols + 2].reshape(4, 2, 2)
        lead_square = gram[:, 0, 0] + epsilon
        lead_root = jnp.sqrt(lead_square)
        correlation = gram[:, 0, 1] / lead_root
        rest = gram[:, 1, 1] - correlation * correlation * (1.0 + epsilon / lead_square)
        rest_root = jnp.sqrt(jnp.maximum(rest, 0.0) + epsilon)
        first = (1.0 / lead_root)[:, None]
        mixed = (-correlation / (lead_root * rest_root))[:, None]
        second = (1.0 / rest_root)[:, None]
        lead_factor = first * raw[:, 0]
        rest_factor = second * raw[:, 1] + mixed * raw[:, 0]
        factors = jnp.stack([lead_factor, rest_factor], 1).reshape(8, local_cols)
        weight = scaling[:, None]
        right = jnp.stack(
            [weight * (first * lead_factor + mixed * rest_factor), weight * second * rest_factor], 1
        ).reshape(8, local_cols)
        lefts.append(left)
        rights.append(right)

    left_high, left_low = two_terms(jnp.concatenate(lefts, 0))
    right_high, right_low = two_terms(jnp.concatenate(rights, 0))
    return lax.dot_general(
        jnp.concatenate([left_high, left_low, left_high], 0),
        jnp.concatenate([right_high, right_high, right_low], 0),
        (((0,), (0,)), ((), ())),
        preferred_element_type=jnp.float32,
    )


def solution(mesh):
    in_specs = (P("row", "col"), P(), P())
    out_specs = P("row", "col")
    return jax.shard_map(
        per_device, mesh=mesh, in_specs=in_specs, out_specs=out_specs, check_vma=False
    )
```

```python
import functools

import jax
import jax.numpy as jnp
from jax import lax
from jax.experimental import pallas as pl
from jax.experimental.pallas import tpu as pltpu
from jax.sharding import PartitionSpec as P

MODULUS_BITS = 13
MODULUS = (1 << MODULUS_BITS) - 1
LANES = 128
CHUNKS = 5

epsilon = 1e-06
over_last = (((1,), (1,)), ((), ()))
over_inner = (((1,), (0,)), ((), ()))
over_first = (((0,), (0,)), ((), ()))


class Layout:
    def __init__(self, graph_rows, graph_cols):
        self.rows, self.cols = lax.axis_size("row"), lax.axis_size("col")
        self.nodes = (graph_rows, graph_cols)
        self.shards = (self.rows // graph_rows, self.cols // graph_cols)

    def exchange(self, value, target):
        pairs = []
        for r in range(self.rows):
            for c in range(self.cols):
                tr, tc = target(r, c)
                pairs.append((r * self.cols + c, tr * self.cols + tc))
        return lax.ppermute(value, ("row", "col"), pairs)

    def row_swap(self, value, bit):
        return self.exchange(value, lambda r, c: (r ^ 1 << bit, c))

    def col_swap(self, value, bit):
        return self.exchange(value, lambda r, c: (r, c ^ 1 << bit))

    def step(self, half, by):
        def target(r, c):
            if (r & 1) == half:
                return (r + by * self.shards[0]) % self.rows, c
            return r, (c + by * self.shards[1]) % self.cols

        return target

    def neighbours(self, value, half):
        if self.nodes == (2, 2):
            return self.exchange(value, self.step(half, 1))
        after = self.exchange(value[2:], self.step(half, -1))
        before = self.exchange(value[:2], self.step(half, 1))
        return jnp.concatenate([after, before], 0)

    def edges(self):
        row_index, col_index = lax.axis_index("row"), lax.axis_index("col")
        node = (row_index // self.shards[0], col_index // self.shards[1])
        found = []
        for half in range(2):
            along_col = (row_index & 1) ^ half
            for slot in range(2):
                owner = []
                for axis in range(2):
                    if self.nodes == (2, 2):
                        mine = slot
                    else:
                        mine = lax.rem(node[axis] + self.nodes[axis] - slot, self.nodes[axis])
                    owner.append(jnp.where(along_col == axis, mine, node[axis]))
                found.append((owner[0], owner[1], along_col))
        return found

    def first_column(self, width):
        return lax.rem(lax.axis_index("col"), self.shards[1]) * width


def stacked(values):
    high = values.astype(jnp.bfloat16).astype(jnp.float32)
    return jnp.concatenate([high, values - high], 0).astype(jnp.bfloat16)


def folded(product):
    half = product.shape[0] // 2
    return product[:half] + product[half:]


def dot(left, right, dims):
    return lax.dot_general(left, right, dims, preferred_element_type=jnp.float32)


def full_product(left, right, dims):
    high = right.astype(jnp.bfloat16)
    low = (right - high.astype(jnp.float32)).astype(jnp.bfloat16)
    terms = stacked(left)
    return folded(dot(terms, high, dims) + dot(terms, low, dims))


def remainder(value):
    value = (value & MODULUS) + (value >> MODULUS_BITS)
    value = (value & MODULUS) + (value >> MODULUS_BITS)
    return jnp.where(value >= MODULUS, value - MODULUS, value)


def row_values(scalars, width):
    rows = lax.broadcasted_iota(jnp.int32, (len(scalars), width), 0)
    values = jnp.full((len(scalars), width), scalars[0], jnp.int32)
    for k in range(1, len(scalars)):
        values = jnp.where(rows == k, scalars[k], values)
    return values


def first_kernel(layout, seeds_ref, counts_ref, replicas_ref, images_ref, scaling_ref):
    edges = layout.edges()
    seeds = row_values([seeds_ref[r, c, a, k] for r, c, a in edges for k in range(2)], LANES)
    counts = row_values([counts_ref[r, c, a] for r, c, a in edges for k in range(2)], LANES)
    scaling_ref[...] = -(counts.astype(jnp.float32) / 16.0)
    width = replicas_ref.shape[1]
    column = layout.first_column(width) + lax.broadcasted_iota(jnp.int32, (8, width), 1)
    square = remainder(column * column)
    residue = remainder(square * (seeds[:, :1] + 1) + column * 17)
    factors = residue.astype(jnp.float32) * (2.0 / MODULUS) - 1.0
    images_ref[...] = folded(dot(stacked(factors), replicas_ref[...], over_last))


def project_kernel(has_update, images_ref, first_ref, second_ref, replicas_ref, *refs):
    if has_update:
        earlier_ref, right_ref, left_ref, keep_ref, send_ref = refs
    else:
        left_ref, keep_ref, send_ref = refs
    left_ref[0:4] = images_ref[0:4] - first_ref[...]
    left_ref[4:8] = images_ref[4:8] - second_ref[...]
    left = left_ref[...]
    width = replicas_ref.shape[1]
    projections = folded(dot(stacked(left), replicas_ref[...], over_inner))
    if has_update:
        cross = full_product(left, earlier_ref[...], over_last)
        projections = projections + full_product(cross, right_ref[...], over_inner)
    rows = lax.broadcasted_iota(jnp.int32, left.shape, 0)
    partner = jnp.where(rows % 2 == 0, pltpu.roll(left, 7, 0), pltpu.roll(left, 1, 0))
    norm = jnp.sum(left * left, 1, keepdims=True)
    inner = jnp.sum(left * partner, 1, keepdims=True)
    lanes = lax.broadcasted_iota(jnp.int32, (8, LANES), 1)
    tail = jnp.where(lanes == 0, norm, inner)
    keep_ref[:, :width] = projections[0:4]
    send_ref[:, :width] = projections[4:8]
    keep_ref[:, width:] = tail[0:4]
    send_ref[:, width:] = tail[4:8]


def orthonormal_factors(mine_ref, other_ref, scaling, total_ref):
    total_ref[0:4] = mine_ref[...]
    total_ref[4:8] = other_ref[...]
    width = total_ref.shape[1] - LANES
    raw = total_ref[:, :width]
    tail = 0.5 * total_ref[:, width:]
    even = lax.broadcasted_iota(jnp.int32, (8, LANES), 0) % 2 == 0
    after, before = pltpu.roll(tail, 7, 0), pltpu.roll(tail, 1, 0)
    lead = jnp.where(even, tail, before)[:, 0:1]
    rest = jnp.where(even, after, tail)[:, 0:1]
    inner = tail[:, 1:2]
    lead_square = lead + epsilon
    lead_root = jnp.sqrt(lead_square)
    correlation = inner / lead_root
    rest = rest - correlation * correlation * (1.0 + epsilon / lead_square)
    rest_root = jnp.sqrt(jnp.maximum(rest, 0.0) + epsilon)
    mixed = -correlation / (lead_root * rest_root)
    even = even[:, 0:1]
    own = jnp.where(even, 1.0 / lead_root, 1.0 / rest_root)
    factors = own * raw + jnp.where(even, 0.0, mixed) * pltpu.roll(raw, 1, 0)
    right = own * factors + jnp.where(even, mixed, 0.0) * pltpu.roll(factors, 7, 0)
    return factors, scaling * right


def images_kernel(mine_ref, other_ref, scaling_ref, left_ref, replicas_ref, images_ref, right_ref, total_ref):
    factors, right = orthonormal_factors(mine_ref, other_ref, scaling_ref[:, 0:1], total_ref)
    right_ref[...] = right
    images = folded(dot(stacked(factors), replicas_ref[...], over_last))
    cross = full_product(factors, right, over_last)
    images_ref[...] = images + full_product(cross, left_ref[...], over_inner)


def update_kernel(
    mine_ref, other_ref, scaling_ref, first_ref, second_ref, right_ref, out_ref, total_ref, terms_ref, block_ref, sems
):
    _, right = orthonormal_factors(mine_ref, other_ref, scaling_ref[:, 0:1], total_ref)
    lefts = jnp.concatenate([first_ref[...], second_ref[...]], 0)
    left_high = lefts.astype(jnp.bfloat16).astype(jnp.float32)
    left_terms = jnp.concatenate([left_high, lefts - left_high, left_high], 0).astype(jnp.bfloat16)
    rights = jnp.concatenate([right_ref[...], right], 0)
    right_high = rights.astype(jnp.bfloat16).astype(jnp.float32)
    terms_ref[...] = jnp.concatenate([right_high, right_high, rights - right_high], 0).astype(
        jnp.bfloat16
    )
    size = block_ref.shape[2]
    copies = []
    for k in range(block_ref.shape[0]):
        columns = pl.ds(k * size, size)
        block_ref[k] = dot(left_terms, terms_ref[:, columns], over_first)
        copies.append(pltpu.make_async_copy(block_ref.at[k], out_ref.at[:, columns], sems.at[k]))
        copies[-1].start()
    for copy in copies:
        copy.wait()


vmem = pl.BlockSpec(memory_space=pltpu.VMEM)
smem = pl.BlockSpec(memory_space=pltpu.SMEM)


def call(kernel, outs, *args, in_specs=None, out_specs=None, scratch=()):
    return pl.pallas_call(
        kernel,
        out_shape=[jax.ShapeDtypeStruct(shape, jnp.float32) for shape in outs],
        in_specs=in_specs or [vmem] * len(args),
        out_specs=out_specs or [vmem] * len(outs),
        scratch_shapes=list(scratch),
        compiler_params=pltpu.CompilerParams(vmem_limit_bytes=16 << 20),
    )(*args)


def per_device(replicas, factor_seeds, edge_counts):
    height, width = replicas.shape
    packed = width + LANES
    layout = Layout(*factor_seeds.shape[:2])
    total_scratch = pltpu.VMEM((8, packed), jnp.float32)

    def reduced(images):
        for bit in range(layout.shards[1].bit_length() - 1):
            images = images + layout.col_swap(images, bit)
        return images, layout.neighbours(images[:4], 0), layout.neighbours(images[4:], 1)

    def summed(keep, send):
        total = keep + layout.row_swap(send, 0)
        for bit in range(1, layout.shards[0].bit_length() - 1):
            total = total + layout.row_swap(total, bit)
        total = total + layout.neighbours(total, 0)
        return total, layout.row_swap(total, 0)

    images, scaling = call(
        functools.partial(first_kernel, layout),
        [(8, height), (8, LANES)],
        factor_seeds,
        edge_counts,
        replicas,
        in_specs=[smem, smem, vmem],
    )
    left_one, keep, send = call(
        functools.partial(project_kernel, False),
        [(8, height), (4, packed), (4, packed)],
        *reduced(images),
        replicas,
    )
    mine, other = summed(keep, send)
    images, right_one = call(
        images_kernel,
        [(8, height), (8, width)],
        mine,
        other,
        scaling,
        left_one,
        replicas,
        scratch=[total_scratch],
    )
    left_two, keep, send = call(
        functools.partial(project_kernel, True),
        [(8, height), (4, packed), (4, packed)],
        *reduced(images),
        replicas,
        left_one,
        right_one,
    )
    mine, other = summed(keep, send)
    (update,) = call(
        update_kernel,
        [(height, width)],
        mine,
        other,
        scaling,
        left_one,
        left_two,
        right_one,
        out_specs=[pl.BlockSpec(memory_space=pl.ANY)],
        scratch=[
            total_scratch,
            pltpu.VMEM((48, width), jnp.bfloat16),
            pltpu.VMEM((CHUNKS, height, width // CHUNKS), jnp.float32),
            pltpu.SemaphoreType.DMA((CHUNKS,)),
        ],
    )
    return update


def solution(mesh):
    in_specs = (P("row", "col"), P(), P())
    out_specs = P("row", "col")
    return jax.shard_map(
        per_device, mesh=mesh, in_specs=in_specs, out_specs=out_specs, check_vma=False
    )
```

```python
import functools

import jax
import jax.numpy as jnp
from jax import lax
from jax.experimental import pallas as pl
from jax.experimental.pallas import tpu as pltpu
from jax.sharding import PartitionSpec as P

MODULUS_BITS = 13
MODULUS = (1 << MODULUS_BITS) - 1
LANES = 128
CHUNKS = 5

epsilon = 1e-06
over_last = (((1,), (1,)), ((), ()))
over_inner = (((1,), (0,)), ((), ()))
over_first = (((0,), (0,)), ((), ()))


class Layout:
    def __init__(self, graph_rows, graph_cols):
        self.rows, self.cols = lax.axis_size("row"), lax.axis_size("col")
        self.nodes = (graph_rows, graph_cols)
        self.shards = (self.rows // graph_rows, self.cols // graph_cols)

    def exchange(self, value, target):
        pairs = []
        for r in range(self.rows):
            for c in range(self.cols):
                tr, tc = target(r, c)
                pairs.append((r * self.cols + c, tr * self.cols + tc))
        return lax.ppermute(value, ("row", "col"), pairs)

    def row_swap(self, value, bit):
        return self.exchange(value, lambda r, c: (r ^ 1 << bit, c))

    def col_swap(self, value, bit):
        return self.exchange(value, lambda r, c: (r, c ^ 1 << bit))

    def step(self, half, by):
        def target(r, c):
            if (r & 1) == half:
                return (r + by * self.shards[0]) % self.rows, c
            return r, (c + by * self.shards[1]) % self.cols

        return target

    def neighbours(self, value, half):
        if self.nodes == (2, 2):
            return self.exchange(value, self.step(half, 1))
        after = self.exchange(value[2:], self.step(half, -1))
        before = self.exchange(value[:2], self.step(half, 1))
        return jnp.concatenate([after, before], 0)

    def edges(self):
        row_index, col_index = lax.axis_index("row"), lax.axis_index("col")
        node = (row_index // self.shards[0], col_index // self.shards[1])
        found = []
        for half in range(2):
            along_col = (row_index & 1) ^ half
            for slot in range(2):
                owner = []
                for axis in range(2):
                    if self.nodes == (2, 2):
                        mine = slot
                    else:
                        mine = lax.rem(node[axis] + self.nodes[axis] - slot, self.nodes[axis])
                    owner.append(jnp.where(along_col == axis, mine, node[axis]))
                found.append((owner[0], owner[1], along_col))
        return found

    def first_column(self, width):
        return lax.rem(lax.axis_index("col"), self.shards[1]) * width


def stacked(values):
    high = values.astype(jnp.bfloat16).astype(jnp.float32)
    return jnp.concatenate([high, values - high], 0).astype(jnp.bfloat16)


def folded(product):
    half = product.shape[0] // 2
    return product[:half] + product[half:]


def dot(left, right, dims):
    return lax.dot_general(left, right, dims, preferred_element_type=jnp.float32)


def full_product(left, right, dims):
    high = right.astype(jnp.bfloat16)
    low = (right - high.astype(jnp.float32)).astype(jnp.bfloat16)
    terms = stacked(left)
    return folded(dot(terms, high, dims) + dot(terms, low, dims))


def remainder(value):
    value = (value & MODULUS) + (value >> MODULUS_BITS)
    value = (value & MODULUS) + (value >> MODULUS_BITS)
    return jnp.where(value >= MODULUS, value - MODULUS, value)


def row_values(scalars, width):
    rows = lax.broadcasted_iota(jnp.int32, (len(scalars), width), 0)
    values = jnp.full((len(scalars), width), scalars[0], jnp.int32)
    for k in range(1, len(scalars)):
        values = jnp.where(rows == k, scalars[k], values)
    return values


def first_kernel(
    layout, seeds_hbm, counts_hbm, replicas_hbm, images_ref, scaling_ref, replicas_ref, seeds_ref, counts_ref, sems
):
    size = replicas_ref.shape[1] // CHUNKS
    blocks = [pl.ds(k * size, size) for k in range(CHUNKS)]
    small = [
        pltpu.make_async_copy(seeds_hbm, seeds_ref, sems.at[CHUNKS]),
        pltpu.make_async_copy(counts_hbm, counts_ref, sems.at[CHUNKS + 1]),
    ]
    copies = [
        pltpu.make_async_copy(replicas_hbm.at[:, block], replicas_ref.at[:, block], sems.at[k])
        for k, block in enumerate(blocks)
    ]
    for copy in small + copies:
        copy.start()
    column = layout.first_column(replicas_ref.shape[1]) + lax.broadcasted_iota(
        jnp.int32, (8, replicas_ref.shape[1]), 1
    )
    square = remainder(column * column)
    edges = layout.edges()
    for copy in small:
        copy.wait()
    seeds = row_values([seeds_ref[r, c, a, k] for r, c, a in edges for k in range(2)], LANES)
    counts = row_values([counts_ref[r, c, a] for r, c, a in edges for k in range(2)], LANES)
    scaling_ref[...] = -(counts.astype(jnp.float32) / 16.0)
    residue = remainder(square * (seeds[:, :1] + 1) + column * 17)
    factors = stacked(residue.astype(jnp.float32) * (2.0 / MODULUS) - 1.0)
    images = 0.0
    for k, block in enumerate(blocks):
        copies[k].wait()
        images = images + dot(factors[:, k * size : (k + 1) * size], replicas_ref[:, block], over_last)
    images_ref[...] = folded(images)


def project_kernel(has_update, images_ref, first_ref, second_ref, replicas_ref, *refs):
    if has_update:
        earlier_ref, right_ref, left_ref, packed_ref = refs
    else:
        left_ref, packed_ref = refs
    left_ref[0:4] = images_ref[0:4] - first_ref[...]
    left_ref[4:8] = images_ref[4:8] - second_ref[...]
    left = left_ref[...]
    width = replicas_ref.shape[1]
    projections = folded(dot(stacked(left), replicas_ref[...], over_inner))
    if has_update:
        cross = full_product(left, earlier_ref[...], over_last)
        projections = projections + full_product(cross, right_ref[...], over_inner)
    rows = lax.broadcasted_iota(jnp.int32, left.shape, 0)
    partner = jnp.where(rows % 2 == 0, pltpu.roll(left, 7, 0), pltpu.roll(left, 1, 0))
    norm = jnp.sum(left * left, 1, keepdims=True)
    inner = jnp.sum(left * partner, 1, keepdims=True)
    lanes = lax.broadcasted_iota(jnp.int32, (8, LANES), 1)
    packed_ref[:, :width] = projections
    packed_ref[:, width:] = jnp.where(lanes == 0, norm, inner)


def coefficients(total_ref, width):
    tail = 0.5 * total_ref[:, width:]
    even = lax.broadcasted_iota(jnp.int32, (8, LANES), 0) % 2 == 0
    after, before = pltpu.roll(tail, 7, 0), pltpu.roll(tail, 1, 0)
    lead = jnp.where(even, tail, before)[:, 0:1]
    rest = jnp.where(even, after, tail)[:, 0:1]
    inner = tail[:, 1:2]
    lead_square = lead + epsilon
    lead_root = jnp.sqrt(lead_square)
    correlation = inner / lead_root
    rest = rest - correlation * correlation * (1.0 + epsilon / lead_square)
    rest_root = jnp.sqrt(jnp.maximum(rest, 0.0) + epsilon)
    mixed = -correlation / (lead_root * rest_root)
    even = even[:, 0:1]
    own = jnp.where(even, 1.0 / lead_root, 1.0 / rest_root)
    return own, jnp.where(even, 0.0, mixed), jnp.where(even, mixed, 0.0)


def right_factors(raw, scaling, own, from_before, from_after):
    factors = own * raw + from_before * pltpu.roll(raw, 1, 0)
    return factors, scaling * (own * factors + from_after * pltpu.roll(factors, 7, 0))


def images_kernel(mine_ref, other_ref, scaling_ref, left_ref, replicas_ref, images_ref, right_ref, total_ref):
    total_ref[0:4] = mine_ref[...]
    total_ref[4:8] = other_ref[...]
    width = replicas_ref.shape[1]
    factors, right = right_factors(
        total_ref[:, :width], scaling_ref[:, 0:1], *coefficients(total_ref, width)
    )
    right_ref[...] = right
    images = folded(dot(stacked(factors), replicas_ref[...], over_last))
    cross = full_product(factors, right, over_last)
    images_ref[...] = images + full_product(cross, left_ref[...], over_inner)


def update_kernel(
    mine_ref, other_ref, scaling_ref, first_ref, second_ref, right_ref, out_ref, total_ref, block_ref, sems
):
    total_ref[0:4] = mine_ref[...]
    total_ref[4:8] = other_ref[...]
    parts = coefficients(total_ref, right_ref.shape[1])
    scaling = scaling_ref[:, 0:1]
    lefts = jnp.concatenate([first_ref[...], second_ref[...]], 0)
    left_high = lefts.astype(jnp.bfloat16).astype(jnp.float32)
    left_terms = jnp.concatenate([left_high, lefts - left_high, left_high], 0).astype(jnp.bfloat16)
    size = block_ref.shape[2]
    copies = []
    for k in range(block_ref.shape[0]):
        columns = pl.ds(k * size, size)
        _, right = right_factors(total_ref[:, columns], scaling, *parts)
        rights = jnp.concatenate([right_ref[:, columns], right], 0)
        right_high = rights.astype(jnp.bfloat16).astype(jnp.float32)
        right_terms = jnp.concatenate([right_high, right_high, rights - right_high], 0)
        block_ref[k] = dot(left_terms, right_terms.astype(jnp.bfloat16), over_first)
        copies.append(pltpu.make_async_copy(block_ref.at[k], out_ref.at[:, columns], sems.at[k]))
        copies[-1].start()
    for copy in copies:
        copy.wait()


vmem = pl.BlockSpec(memory_space=pltpu.VMEM)
hbm = pl.BlockSpec(memory_space=pltpu.HBM)


def call(kernel, outs, *args, in_specs=None, out_specs=None, scratch=()):
    return pl.pallas_call(
        kernel,
        out_shape=outs,
        in_specs=in_specs or [vmem] * len(args),
        out_specs=out_specs or [vmem] * len(outs),
        scratch_shapes=list(scratch),
        compiler_params=pltpu.CompilerParams(vmem_limit_bytes=16 << 20),
    )(*args)


def single(*shape):
    return jax.ShapeDtypeStruct(shape, jnp.float32)


def per_device(replicas_hbm, factor_seeds, edge_counts):
    height, width = replicas_hbm.shape
    packed = width + LANES
    layout = Layout(*factor_seeds.shape[:2])
    total_scratch = pltpu.VMEM((8, packed), jnp.float32)

    def reduced(images):
        for bit in range(layout.shards[1].bit_length() - 1):
            images = images + layout.col_swap(images, bit)
        return images, layout.neighbours(images[:4], 0), layout.neighbours(images[4:], 1)

    def summed(values):
        other = layout.row_swap(values, 0)
        total, rest = values[:4] + other[4:], values[4:] + other[:4]
        if layout.shards[0] > 2:
            total = total + layout.exchange(rest, lambda r, c: (r ^ 3, c))
        for bit in range(2, layout.shards[0].bit_length() - 1):
            total = total + layout.row_swap(total, bit)
        total = total + layout.neighbours(total, 0)
        return total, layout.row_swap(total, 0)

    images, scaling, replicas = call(
        functools.partial(first_kernel, layout),
        [single(8, height), single(8, LANES), jax.ShapeDtypeStruct((height, width), replicas_hbm.dtype)],
        *(pltpu.with_memory_space_constraint(array, pltpu.HBM) for array in (factor_seeds, edge_counts, replicas_hbm)),
        in_specs=[hbm] * 3,
        scratch=[
            pltpu.SMEM(factor_seeds.shape, jnp.int32),
            pltpu.SMEM(edge_counts.shape, jnp.int32),
            pltpu.SemaphoreType.DMA((CHUNKS + 2,)),
        ],
    )
    left_one, values = call(
        functools.partial(project_kernel, False),
        [single(8, height), single(8, packed)],
        *reduced(images),
        replicas,
    )
    images, right_one = call(
        images_kernel,
        [single(8, height), single(8, width)],
        *summed(values),
        scaling,
        left_one,
        replicas,
        scratch=[total_scratch],
    )
    left_two, values = call(
        functools.partial(project_kernel, True),
        [single(8, height), single(8, packed)],
        *reduced(images),
        replicas,
        left_one,
        right_one,
    )
    (update,) = call(
        update_kernel,
        [single(height, width)],
        *summed(values),
        scaling,
        left_one,
        left_two,
        right_one,
        out_specs=[hbm],
        scratch=[
            total_scratch,
            pltpu.VMEM((CHUNKS, height, width // CHUNKS), jnp.float32),
            pltpu.SemaphoreType.DMA((CHUNKS,)),
        ],
    )
    return update


def solution(mesh):
    in_specs = (P("row", "col"), P(), P())
    out_specs = P("row", "col")
    return jax.shard_map(
        per_device, mesh=mesh, in_specs=in_specs, out_specs=out_specs, check_vma=False
    )
```

```python
import functools

import jax
import jax.numpy as jnp
from jax import lax
from jax.experimental import pallas as pl
from jax.experimental.pallas import tpu as pltpu
from jax.sharding import PartitionSpec as P

MODULUS_BITS = 13
MODULUS = (1 << MODULUS_BITS) - 1
LANES = 128
CHUNKS = 5

epsilon = 1e-06
over_last = (((1,), (1,)), ((), ()))
over_inner = (((1,), (0,)), ((), ()))
over_first = (((0,), (0,)), ((), ()))


class Layout:
    def __init__(self, graph_rows, graph_cols):
        self.rows, self.cols = lax.axis_size("row"), lax.axis_size("col")
        self.nodes = (graph_rows, graph_cols)
        self.shards = (self.rows // graph_rows, self.cols // graph_cols)

    def exchange(self, value, target):
        pairs = []
        for r in range(self.rows):
            for c in range(self.cols):
                tr, tc = target(r, c)
                pairs.append((r * self.cols + c, tr * self.cols + tc))
        return lax.ppermute(value, ("row", "col"), pairs)

    def row_swap(self, value, bit):
        return self.exchange(value, lambda r, c: (r ^ 1 << bit, c))

    def col_swap(self, value, bit):
        return self.exchange(value, lambda r, c: (r, c ^ 1 << bit))

    def step(self, half, by):
        def target(r, c):
            if (r & 1) == half:
                return (r + by * self.shards[0]) % self.rows, c
            return r, (c + by * self.shards[1]) % self.cols

        return target

    def neighbours(self, value, half):
        if self.nodes == (2, 2):
            return self.exchange(value, self.step(half, 1))
        fours = value.reshape(-1, 2, 2, value.shape[1])
        after = self.exchange(fours[:, 1], self.step(half, -1))
        before = self.exchange(fours[:, 0], self.step(half, 1))
        return jnp.stack([after, before], 1).reshape(value.shape)

    def edges(self):
        row_index, col_index = lax.axis_index("row"), lax.axis_index("col")
        node = (row_index // self.shards[0], col_index // self.shards[1])
        found = []
        for half in range(2):
            along_col = (row_index & 1) ^ half
            for slot in range(2):
                owner = []
                for axis in range(2):
                    if self.nodes == (2, 2):
                        mine = slot
                    else:
                        mine = lax.rem(node[axis] + self.nodes[axis] - slot, self.nodes[axis])
                    owner.append(jnp.where(along_col == axis, mine, node[axis]))
                found.append((owner[0], owner[1], along_col))
        return found

    def first_column(self, width):
        return lax.rem(lax.axis_index("col"), self.shards[1]) * width


def stacked(values):
    high = values.astype(jnp.bfloat16).astype(jnp.float32)
    return jnp.concatenate([high, values - high], 0).astype(jnp.bfloat16)


def folded(product):
    half = product.shape[0] // 2
    return product[:half] + product[half:]


def dot(left, right, dims):
    return lax.dot_general(left, right, dims, preferred_element_type=jnp.float32)


def full_product(left, right, dims):
    high = right.astype(jnp.bfloat16)
    low = (right - high.astype(jnp.float32)).astype(jnp.bfloat16)
    terms = stacked(left)
    return folded(dot(terms, high, dims) + dot(terms, low, dims))


def remainder(value):
    value = (value & MODULUS) + (value >> MODULUS_BITS)
    value = (value & MODULUS) + (value >> MODULUS_BITS)
    return jnp.where(value >= MODULUS, value - MODULUS, value)


def row_values(scalars, width):
    rows = lax.broadcasted_iota(jnp.int32, (len(scalars), width), 0)
    values = jnp.full((len(scalars), width), scalars[0], jnp.int32)
    for k in range(1, len(scalars)):
        values = jnp.where(rows == k, scalars[k], values)
    return values


def first_kernel(
    layout, seeds_hbm, counts_hbm, replicas_hbm, keep_ref, send_ref, scaling_ref, replicas_ref, seeds_ref, counts_ref, sems
):
    size = replicas_ref.shape[1] // CHUNKS
    blocks = [pl.ds(k * size, size) for k in range(CHUNKS)]
    small = [
        pltpu.make_async_copy(seeds_hbm, seeds_ref, sems.at[CHUNKS]),
        pltpu.make_async_copy(counts_hbm, counts_ref, sems.at[CHUNKS + 1]),
    ]
    copies = [
        pltpu.make_async_copy(replicas_hbm.at[:, block], replicas_ref.at[:, block], sems.at[k])
        for k, block in enumerate(blocks)
    ]
    for copy in small + copies:
        copy.start()
    column = layout.first_column(replicas_ref.shape[1]) + lax.broadcasted_iota(
        jnp.int32, (8, replicas_ref.shape[1]), 1
    )
    square = remainder(column * column)
    edges = layout.edges()
    for copy in small:
        copy.wait()
    seeds = row_values([seeds_ref[r, c, a, k] for r, c, a in edges for k in range(2)], LANES)
    counts = row_values([counts_ref[r, c, a] for r, c, a in edges for k in range(2)], LANES)
    scaling_ref[...] = -(counts.astype(jnp.float32) / 16.0)
    residue = remainder(square * (seeds[:, :1] + 1) + column * 17)
    factors = stacked(residue.astype(jnp.float32) * (2.0 / MODULUS) - 1.0)
    images = 0.0
    for k, block in enumerate(blocks):
        copies[k].wait()
        images = images + dot(factors[:, k * size : (k + 1) * size], replicas_ref[:, block], over_last)
    images = folded(images)
    keep_ref[...] = images[0:4]
    send_ref[...] = images[4:8]


def widen_kernel(values_ref, out_ref):
    out_ref[...] = values_ref[...].astype(jnp.float32)


def narrow_kernel(values_ref, out_ref):
    out_ref[...] = values_ref[...].astype(jnp.bfloat16)


def upper(shape):
    return lax.broadcasted_iota(jnp.int32, shape, 0) < 4


def halves_added(values):
    return values + pltpu.roll(values, 4, 0)


def project_kernel(has_update, images_ref, neighbour_ref, mine_ref, pair_ref, *refs):
    if has_update:
        mine_left_ref, pair_left_ref, right_ref, left_ref, packed_ref, wide_ref = refs
    else:
        left_ref, packed_ref, wide_ref = refs
    left = images_ref[...] - neighbour_ref[...]
    left_ref[...] = left
    height, width = mine_ref.shape
    wide_ref[:, :height] = left[0:4]
    wide_ref[:, wide_ref.shape[1] // 2 : wide_ref.shape[1] // 2 + height] = left[4:8]
    terms = stacked(left)
    projections = jnp.where(
        upper((8, width)),
        folded(dot(terms, mine_ref[...], over_inner)),
        folded(dot(terms, pair_ref[...], over_inner)),
    )
    if has_update:
        cross = jnp.where(
            upper((8, 8)),
            full_product(left, mine_left_ref[...], over_last),
            full_product(left, pair_left_ref[...], over_last),
        )
        projections = projections + full_product(cross, right_ref[...], over_inner)
    rows = lax.broadcasted_iota(jnp.int32, left.shape, 0)
    partner = jnp.where(rows % 2 == 0, pltpu.roll(left, 7, 0), pltpu.roll(left, 1, 0))
    norm = jnp.sum(left * left, 1, keepdims=True)
    inner = jnp.sum(left * partner, 1, keepdims=True)
    lanes = lax.broadcasted_iota(jnp.int32, (8, LANES), 1)
    packed_ref[:, :width] = halves_added(projections)[0:4]
    packed_ref[:, width:] = halves_added(jnp.where(lanes == 0, norm, inner))[0:4]


def coefficients(total_ref, width):
    tail = 0.5 * total_ref[:, width:]
    even = lax.broadcasted_iota(jnp.int32, (8, LANES), 0) % 2 == 0
    after, before = pltpu.roll(tail, 7, 0), pltpu.roll(tail, 1, 0)
    lead = jnp.where(even, tail, before)[:, 0:1]
    rest = jnp.where(even, after, tail)[:, 0:1]
    inner = tail[:, 1:2]
    lead_square = lead + epsilon
    lead_root = jnp.sqrt(lead_square)
    correlation = inner / lead_root
    rest = rest - correlation * correlation * (1.0 + epsilon / lead_square)
    rest_root = jnp.sqrt(jnp.maximum(rest, 0.0) + epsilon)
    mixed = -correlation / (lead_root * rest_root)
    even = even[:, 0:1]
    own = jnp.where(even, 1.0 / lead_root, 1.0 / rest_root)
    return own, jnp.where(even, 0.0, mixed), jnp.where(even, mixed, 0.0)


def right_factors(raw, scaling, own, from_before, from_after):
    factors = own * raw + from_before * pltpu.roll(raw, 1, 0)
    return factors, scaling * (own * factors + from_after * pltpu.roll(factors, 7, 0))


def own_kernel(mine_ref, scaling_ref, replicas_ref, pair_ref, images_ref, factors_ref, right_ref, total_ref):
    width = replicas_ref.shape[1]
    total_ref[0:4] = mine_ref[:, : width + LANES]
    total_ref[4:8] = mine_ref[:, : width + LANES]
    factors, right = right_factors(
        total_ref[:, :width], scaling_ref[:, 0:1], *coefficients(total_ref, width)
    )
    factors_ref[...] = factors
    right_ref[...] = right[0:4]
    high = factors.astype(jnp.bfloat16).astype(jnp.float32)
    terms = jnp.where(upper(factors.shape), high, factors - high).astype(jnp.bfloat16)
    images = halves_added(dot(terms, replicas_ref[...], over_last))
    pair_images = halves_added(dot(terms, pair_ref[...], over_last))
    images_ref[...] = jnp.where(upper(images.shape), images, pair_images)


def images_kernel(
    other_ref, scaling_ref, left_ref, partial_ref, factors_ref, own_right_ref,
    images_ref, mine_left_ref, pair_left_ref, right_ref, total_ref,
):
    height, width = left_ref.shape[1], factors_ref.shape[1]
    total_ref[0:4] = other_ref[:, : width + LANES]
    total_ref[4:8] = other_ref[:, : width + LANES]
    _, right = right_factors(
        total_ref[:, :width], scaling_ref[:, 0:1], *coefficients(total_ref, width)
    )
    right_ref[0:4] = own_right_ref[...]
    right_ref[4:8] = right[4:8]
    first = width + LANES
    second = first + (other_ref.shape[1] - first) // 2
    mine_left_ref[0:4] = left_ref[0:4]
    mine_left_ref[4:8] = other_ref[:, second : second + height]
    pair_left_ref[0:4] = left_ref[4:8]
    pair_left_ref[4:8] = other_ref[:, first : first + height]
    cross = full_product(factors_ref[...], right_ref[...], over_last)
    images_ref[...] = partial_ref[...] + jnp.where(
        upper((8, height)),
        full_product(cross, mine_left_ref[...], over_inner),
        full_product(cross, pair_left_ref[...], over_inner),
    )


def update_kernel(
    mine_ref, other_ref, scaling_ref, first_ref, left_ref, right_ref, out_ref, total_ref, second_ref, block_ref, sems
):
    height, width = left_ref.shape[1], right_ref.shape[1]
    packed = width + LANES
    total_ref[0:4] = mine_ref[:, :packed]
    total_ref[4:8] = other_ref[:, :packed]
    start = packed + (other_ref.shape[1] - packed) // 2
    second_ref[0:4] = left_ref[0:4]
    second_ref[4:8] = other_ref[:, start : start + height]
    parts = coefficients(total_ref, width)
    scaling = scaling_ref[:, 0:1]
    lefts = jnp.concatenate([first_ref[...], second_ref[...]], 0)
    left_high = lefts.astype(jnp.bfloat16).astype(jnp.float32)
    left_terms = jnp.concatenate([left_high, lefts - left_high, left_high], 0).astype(jnp.bfloat16)
    size = block_ref.shape[2]
    copies = []
    for k in range(block_ref.shape[0]):
        columns = pl.ds(k * size, size)
        _, right = right_factors(total_ref[:, columns], scaling, *parts)
        rights = jnp.concatenate([right_ref[:, columns], right], 0)
        right_high = rights.astype(jnp.bfloat16).astype(jnp.float32)
        right_terms = jnp.concatenate([right_high, right_high, rights - right_high], 0)
        block_ref[k] = dot(left_terms, right_terms.astype(jnp.bfloat16), over_first)
        copies.append(pltpu.make_async_copy(block_ref.at[k], out_ref.at[:, columns], sems.at[k]))
        copies[-1].start()
    for copy in copies:
        copy.wait()


vmem = pl.BlockSpec(memory_space=pltpu.VMEM)
hbm = pl.BlockSpec(memory_space=pltpu.HBM)


def call(kernel, outs, *args, in_specs=None, out_specs=None, scratch=(), work=0):
    return pl.pallas_call(
        kernel,
        out_shape=outs,
        in_specs=in_specs or [vmem] * len(args),
        out_specs=out_specs or [vmem] * len(outs),
        scratch_shapes=list(scratch),
        compiler_params=pltpu.CompilerParams(vmem_limit_bytes=16 << 20),
        cost_estimate=pl.CostEstimate(flops=work, bytes_accessed=work, transcendentals=0),
    )(*args)


def single(*shape):
    return jax.ShapeDtypeStruct(shape, jnp.float32)


def per_device(replicas_hbm, factor_seeds, edge_counts):
    height, width = replicas_hbm.shape
    packed = width + LANES
    wide = 2 * (-(-height // LANES) * LANES)
    layout = Layout(*factor_seeds.shape[:2])
    total_scratch = pltpu.VMEM((8, packed), jnp.float32)
    work = replicas_hbm.size

    def reduced(images):
        for bit in range(layout.shards[1].bit_length() - 1):
            images = images + layout.col_swap(images, bit)
        return images, layout.neighbours(images, 0)

    def summed(total, left):
        for bit in range(1, layout.shards[0].bit_length() - 1):
            total = total + layout.row_swap(total, bit)
        total = jnp.concatenate([total + layout.neighbours(total, 0), left], 1)
        return total, layout.row_swap(total, 0)

    keep, send, scaling, replicas = call(
        functools.partial(first_kernel, layout),
        [
            single(4, height),
            single(4, height),
            single(8, LANES),
            jax.ShapeDtypeStruct((height, width), replicas_hbm.dtype),
        ],
        *(
            pltpu.with_memory_space_constraint(array, pltpu.HBM)
            for array in (factor_seeds, edge_counts, replicas_hbm)
        ),
        in_specs=[hbm] * 3,
        scratch=[
            pltpu.SMEM(factor_seeds.shape, jnp.int32),
            pltpu.SMEM(edge_counts.shape, jnp.int32),
            pltpu.SemaphoreType.DMA((CHUNKS + 2,)),
        ],
        work=work,
    )
    images = jnp.concatenate([keep, layout.row_swap(send, 0)], 0)
    (widened,) = call(widen_kernel, [single(height, width)], replicas, work=work)
    images, widened = lax.optimization_barrier((images, widened))
    swapped = layout.row_swap(widened, 0)
    (pair,) = call(
        narrow_kernel, [jax.ShapeDtypeStruct((height, width), replicas_hbm.dtype)], swapped, work=work
    )
    left_one, values, wide_left = call(
        functools.partial(project_kernel, False),
        [single(8, height), single(4, packed), single(4, wide)],
        *reduced(images),
        replicas,
        pair,
        work=work,
    )
    mine, other = summed(values, wide_left)
    partial, factors, right_one = call(
        own_kernel,
        [single(8, height), single(8, width), single(4, width)],
        mine,
        scaling,
        replicas,
        pair,
        scratch=[total_scratch],
        work=work,
    )
    images, mine_left, pair_left, right_one = call(
        images_kernel,
        [single(8, height), single(8, height), single(8, height), single(8, width)],
        other,
        scaling,
        left_one,
        partial,
        factors,
        right_one,
        scratch=[total_scratch],
        work=work,
    )
    left_two, values, wide_left = call(
        functools.partial(project_kernel, True),
        [single(8, height), single(4, packed), single(4, wide)],
        *reduced(images),
        replicas,
        pair,
        mine_left,
        pair_left,
        right_one,
        work=work,
    )
    (update,) = call(
        update_kernel,
        [single(height, width)],
        *summed(values, wide_left),
        scaling,
        mine_left,
        left_two,
        right_one,
        out_specs=[hbm],
        scratch=[
            total_scratch,
            pltpu.VMEM((8, height), jnp.float32),
            pltpu.VMEM((CHUNKS, height, width // CHUNKS), jnp.float32),
            pltpu.SemaphoreType.DMA((CHUNKS,)),
        ],
        work=work,
    )
    return update


def solution(mesh):
    in_specs = (P("row", "col"), P(), P())
    out_specs = P("row", "col")
    return jax.shard_map(
        per_device, mesh=mesh, in_specs=in_specs, out_specs=out_specs, check_vma=False
    )
```

```python
import functools

import jax
import jax.numpy as jnp
from jax import lax
from jax.experimental import pallas as pl
from jax.experimental.pallas import tpu as pltpu
from jax.sharding import PartitionSpec as P

MODULUS_BITS = 13
MODULUS = (1 << MODULUS_BITS) - 1
LANES = 128
CHUNKS = 5

epsilon = 1e-06
over_last = (((1,), (1,)), ((), ()))
over_inner = (((1,), (0,)), ((), ()))


class Layout:
    def __init__(self, graph_rows, graph_cols):
        self.rows, self.cols = lax.axis_size("row"), lax.axis_size("col")
        self.nodes = (graph_rows, graph_cols)
        self.shards = (self.rows // graph_rows, self.cols // graph_cols)

    def exchange(self, value, target):
        pairs = []
        for r in range(self.rows):
            for c in range(self.cols):
                tr, tc = target(r, c)
                pairs.append((r * self.cols + c, tr * self.cols + tc))
        return lax.ppermute(value, ("row", "col"), pairs)

    def row_swap(self, value, bit):
        return self.exchange(value, lambda r, c: (r ^ 1 << bit, c))

    def col_swap(self, value, bit):
        return self.exchange(value, lambda r, c: (r, c ^ 1 << bit))

    def step(self, half, by):
        def target(r, c):
            if (r & 1) == half:
                return (r + by * self.shards[0]) % self.rows, c
            return r, (c + by * self.shards[1]) % self.cols

        return target

    def neighbours(self, value, half):
        if self.nodes == (2, 2):
            return self.exchange(value, self.step(half, 1))
        fours = value.reshape(-1, 2, 2, value.shape[1])
        after = self.exchange(fours[:, 1], self.step(half, -1))
        before = self.exchange(fours[:, 0], self.step(half, 1))
        return jnp.stack([after, before], 1).reshape(value.shape)

    def edges(self):
        row_index, col_index = lax.axis_index("row"), lax.axis_index("col")
        node = (row_index // self.shards[0], col_index // self.shards[1])
        found = []
        for half in range(2):
            along_col = (row_index & 1) ^ half
            for slot in range(2):
                owner = []
                for axis in range(2):
                    if self.nodes == (2, 2):
                        mine = slot
                    else:
                        mine = lax.rem(node[axis] + self.nodes[axis] - slot, self.nodes[axis])
                    owner.append(jnp.where(along_col == axis, mine, node[axis]))
                found.append((owner[0], owner[1], along_col))
        return found

    def first_column(self, width):
        return lax.rem(lax.axis_index("col"), self.shards[1]) * width


def stacked(values):
    high = values.astype(jnp.bfloat16).astype(jnp.float32)
    return jnp.concatenate([high, values - high], 0).astype(jnp.bfloat16)


def folded(product):
    half = product.shape[0] // 2
    return product[:half] + product[half:]


def dot(left, right, dims):
    return lax.dot_general(left, right, dims, preferred_element_type=jnp.float32)


def full_product(left, right, dims):
    high = right.astype(jnp.bfloat16)
    low = (right - high.astype(jnp.float32)).astype(jnp.bfloat16)
    terms = stacked(left)
    return folded(dot(terms, high, dims) + dot(terms, low, dims))


def remainder(value):
    value = (value & MODULUS) + (value >> MODULUS_BITS)
    value = (value & MODULUS) + (value >> MODULUS_BITS)
    return jnp.where(value >= MODULUS, value - MODULUS, value)


def row_values(scalars, width):
    rows = lax.broadcasted_iota(jnp.int32, (len(scalars), width), 0)
    values = jnp.full((len(scalars), width), scalars[0], jnp.int32)
    for k in range(1, len(scalars)):
        values = jnp.where(rows == k, scalars[k], values)
    return values


def first_kernel(
    layout, seeds_hbm, counts_hbm, replicas_hbm, keep_ref, send_ref, scaling_ref, replicas_ref, seeds_ref, counts_ref, sems
):
    size = replicas_ref.shape[1] // CHUNKS
    blocks = [pl.ds(k * size, size) for k in range(CHUNKS)]
    small = [
        pltpu.make_async_copy(seeds_hbm, seeds_ref, sems.at[CHUNKS]),
        pltpu.make_async_copy(counts_hbm, counts_ref, sems.at[CHUNKS + 1]),
    ]
    copies = [
        pltpu.make_async_copy(replicas_hbm.at[:, block], replicas_ref.at[:, block], sems.at[k])
        for k, block in enumerate(blocks)
    ]
    for copy in small + copies:
        copy.start()
    column = layout.first_column(replicas_ref.shape[1]) + lax.broadcasted_iota(
        jnp.int32, (8, replicas_ref.shape[1]), 1
    )
    square = remainder(column * column)
    edges = layout.edges()
    for copy in small:
        copy.wait()
    seeds = row_values([seeds_ref[r, c, a, k] for r, c, a in edges for k in range(2)], LANES)
    counts = row_values([counts_ref[r, c, a] for r, c, a in edges for _ in range(2)], LANES)
    scaling_ref[...] = -(counts.astype(jnp.float32) / 16.0)
    residue = remainder(square * (seeds[:, :1] + 1) + column * 17)
    factors = stacked(residue.astype(jnp.float32) * (2.0 / MODULUS) - 1.0)
    images = 0.0
    for k, block in enumerate(blocks):
        copies[k].wait()
        images = images + dot(factors[:, k * size : (k + 1) * size], replicas_ref[:, block], over_last)
    images = folded(images)
    keep_ref[...] = images[0:4]
    send_ref[...] = images[4:8]


def widen_kernel(values_ref, out_ref):
    out_ref[...] = values_ref[...].astype(jnp.float32)


def narrow_kernel(mine_ref, values_ref, out_ref):
    height = mine_ref.shape[0]
    out_ref[:height] = mine_ref[...]
    out_ref[height:] = values_ref[...].astype(jnp.bfloat16)


def upper(shape):
    return lax.broadcasted_iota(jnp.int32, shape, 0) < 4


def halves_added(values):
    return values + pltpu.roll(values, 4, 0)


def project_kernel(has_update, images_ref, neighbour_ref, both_ref, *refs):
    if has_update:
        mine_left_ref, pair_left_ref, right_ref, left_ref, packed_ref, wide_ref, terms_ref = refs
    else:
        left_ref, packed_ref, wide_ref, terms_ref = refs
    left = images_ref[...] - neighbour_ref[...]
    left_ref[...] = left
    height, width = left.shape[1], both_ref.shape[1]
    wide_ref[:, :height] = left[0:4]
    wide_ref[:, wide_ref.shape[1] // 2 : wide_ref.shape[1] // 2 + height] = left[4:8]
    high = left.astype(jnp.bfloat16).astype(jnp.float32)
    low = left - high
    terms_ref[:, :height] = jnp.where(upper(left.shape), high, pltpu.roll(low, 4, 0))
    terms_ref[:, height:] = jnp.where(upper(left.shape), pltpu.roll(high, 4, 0), low)
    projections = dot(terms_ref[...].astype(jnp.bfloat16), both_ref[...], over_inner)
    if has_update:
        cross = jnp.where(
            upper((8, 8)),
            full_product(left, mine_left_ref[...], over_last),
            full_product(left, pair_left_ref[...], over_last),
        )
        projections = projections + full_product(cross, right_ref[:, :width], over_inner)
    rows = lax.broadcasted_iota(jnp.int32, left.shape, 0)
    partner = jnp.where(rows % 2 == 0, pltpu.roll(left, 7, 0), pltpu.roll(left, 1, 0))
    norm = jnp.sum(left * left, 1, keepdims=True)
    inner = jnp.sum(left * partner, 1, keepdims=True)
    lanes = lax.broadcasted_iota(jnp.int32, (8, LANES), 1)
    packed_ref[:, :width] = halves_added(projections)[0:4]
    packed_ref[:, width:] = halves_added(jnp.where(lanes == 0, norm, inner))[0:4]


def coefficients(total_ref, width):
    tail = 0.5 * total_ref[:, width:]
    even = lax.broadcasted_iota(jnp.int32, (8, LANES), 0) % 2 == 0
    after, before = pltpu.roll(tail, 7, 0), pltpu.roll(tail, 1, 0)
    lead = jnp.where(even, tail, before)[:, 0:1]
    rest = jnp.where(even, after, tail)[:, 0:1]
    inner = tail[:, 1:2]
    lead_square = lead + epsilon
    lead_root = jnp.sqrt(lead_square)
    correlation = inner / lead_root
    rest = rest - correlation * correlation * (1.0 + epsilon / lead_square)
    rest_root = jnp.sqrt(jnp.maximum(rest, 0.0) + epsilon)
    mixed = -correlation / (lead_root * rest_root)
    even = even[:, 0:1]
    own = jnp.where(even, 1.0 / lead_root, 1.0 / rest_root)
    return own, jnp.where(even, 0.0, mixed), jnp.where(even, mixed, 0.0)


def rotated(raw, own, from_before):
    return own * raw + from_before * pltpu.roll(raw, 1, 0)


def weighted(left, scaling, own, from_before, from_after):
    turned = rotated(left, own, from_before)
    return scaling * (own * turned + from_after * pltpu.roll(turned, 7, 0))


def own_kernel(mine_ref, both_ref, images_ref, factors_ref, total_ref):
    height, width = images_ref.shape[1], both_ref.shape[1]
    total_ref[0:4] = mine_ref[:, : width + LANES]
    total_ref[4:8] = mine_ref[:, : width + LANES]
    own, from_before, _ = coefficients(total_ref, width)
    factors = rotated(total_ref[:, :width], own, from_before)
    high = factors.astype(jnp.bfloat16).astype(jnp.float32)
    terms = jnp.where(upper(factors.shape), high, factors - high).astype(jnp.bfloat16)
    factors_ref[...] = factors
    images = halves_added(dot(terms, both_ref[...], over_last))
    images_ref[...] = jnp.where(
        upper((8, height)), images[:, :height], images[:, height : 2 * height]
    )


def images_kernel(
    mine_ref, other_ref, scaling_ref, left_ref, partial_ref, factors_ref,
    images_ref, mine_left_ref, pair_left_ref, total_ref,
):
    height, width = left_ref.shape[1], factors_ref.shape[1]
    first = width + LANES
    second = first + (other_ref.shape[1] - first) // 2
    total_ref[0:4] = mine_ref[:, :first]
    total_ref[4:8] = other_ref[:, :first]
    cross = folded(dot(stacked(factors_ref[...]), stacked(total_ref[:, :width]), over_last))
    mine_left_ref[0:4] = left_ref[0:4]
    mine_left_ref[4:8] = other_ref[:, second : second + height]
    pair_left_ref[0:4] = left_ref[4:8]
    pair_left_ref[4:8] = other_ref[:, first : first + height]
    parts = coefficients(total_ref, width)
    scaling = scaling_ref[:, 0:1]
    mine_left = weighted(mine_left_ref[...], scaling, *parts)
    pair_left = weighted(pair_left_ref[...], scaling, *parts)
    mine_left_ref[...] = mine_left
    pair_left_ref[...] = pair_left
    images_ref[...] = partial_ref[...] + jnp.where(
        upper((8, height)),
        full_product(cross, jnp.concatenate([mine_left] * 2, 0), over_inner),
        full_product(cross, jnp.concatenate([pair_left] * 2, 0), over_inner),
    )


def update_kernel(
    mine_ref, other_ref, scaling_ref, first_ref, left_ref, right_ref, out_ref, total_ref, second_ref, block_ref, sems
):
    height, width = left_ref.shape[1], out_ref.shape[1]
    packed = width + LANES
    total_ref[0:4] = mine_ref[:, :packed]
    total_ref[4:8] = other_ref[:, :packed]
    start = packed + (other_ref.shape[1] - packed) // 2
    second_ref[0:4] = left_ref[0:4]
    second_ref[4:8] = other_ref[:, start : start + height]
    second = weighted(second_ref[...], scaling_ref[:, 0:1], *coefficients(total_ref, width))
    lefts = jnp.concatenate([first_ref[...], second], 0)
    left_high = lefts.astype(jnp.bfloat16).astype(jnp.float32)
    left_terms = jnp.concatenate([left_high, lefts - left_high, left_high], 0).T.astype(jnp.bfloat16)
    size = block_ref.shape[2]
    copies = []
    for k in range(block_ref.shape[0]):
        columns = pl.ds(k * size, size)
        rights = jnp.concatenate([right_ref[:, columns], total_ref[:, columns]], 0)
        right_high = rights.astype(jnp.bfloat16).astype(jnp.float32)
        right_terms = jnp.concatenate([right_high, right_high, rights - right_high], 0)
        block_ref[k] = dot(left_terms, right_terms.astype(jnp.bfloat16), over_inner)
        copies.append(pltpu.make_async_copy(block_ref.at[k], out_ref.at[:, columns], sems.at[k]))
        copies[-1].start()
    for copy in copies:
        copy.wait()


vmem = pl.BlockSpec(memory_space=pltpu.VMEM)
hbm = pl.BlockSpec(memory_space=pltpu.HBM)


def call(kernel, outs, *args, in_specs=None, out_specs=None, scratch=(), work=0):
    return pl.pallas_call(
        kernel,
        out_shape=outs,
        in_specs=in_specs or [vmem] * len(args),
        out_specs=out_specs or [vmem] * len(outs),
        scratch_shapes=list(scratch),
        compiler_params=pltpu.CompilerParams(vmem_limit_bytes=16 << 20),
        cost_estimate=pl.CostEstimate(flops=work, bytes_accessed=work, transcendentals=0),
    )(*args)


def single(*shape):
    return jax.ShapeDtypeStruct(shape, jnp.float32)


def per_device(replicas_hbm, factor_seeds, edge_counts):
    height, width = replicas_hbm.shape
    packed = width + LANES
    wide = 2 * (-(-height // LANES) * LANES)
    layout = Layout(*factor_seeds.shape[:2])
    total_scratch = pltpu.VMEM((8, packed), jnp.float32)
    work = replicas_hbm.size

    def reduced(images):
        for bit in range(layout.shards[1].bit_length() - 1):
            images = images + layout.col_swap(images, bit)
        return images, layout.neighbours(images, 0)

    def summed(total, left):
        for bit in range(1, layout.shards[0].bit_length() - 1):
            total = total + layout.row_swap(total, bit)
        total = jnp.concatenate([total + layout.neighbours(total, 0), left], 1)
        return total, layout.row_swap(total, 0)

    keep, send, scaling, replicas = call(
        functools.partial(first_kernel, layout),
        [
            single(4, height),
            single(4, height),
            single(8, LANES),
            jax.ShapeDtypeStruct((height, width), replicas_hbm.dtype),
        ],
        *(
            pltpu.with_memory_space_constraint(array, pltpu.HBM)
            for array in (factor_seeds, edge_counts, replicas_hbm)
        ),
        in_specs=[hbm] * 3,
        scratch=[
            pltpu.SMEM(factor_seeds.shape, jnp.int32),
            pltpu.SMEM(edge_counts.shape, jnp.int32),
            pltpu.SemaphoreType.DMA((CHUNKS + 2,)),
        ],
        work=work,
    )
    taken = layout.row_swap(send, 0)
    images = jnp.concatenate([keep, taken], 0)
    (widened,) = call(widen_kernel, [single(height, width)], replicas, work=work)
    swapped = layout.row_swap(widened, 0)
    (both,) = call(
        narrow_kernel,
        [jax.ShapeDtypeStruct((2 * height, width), replicas_hbm.dtype)],
        replicas,
        swapped,
        work=work,
    )
    terms_scratch = pltpu.VMEM((8, 2 * height), jnp.float32)
    left_one, values, wide_left = call(
        functools.partial(project_kernel, False),
        [single(8, height), single(4, packed), single(4, wide)],
        *reduced(images),
        both,
        scratch=[terms_scratch],
        work=work,
    )
    mine, other = summed(values, wide_left)
    partial, factors = call(
        own_kernel,
        [single(8, height), single(8, width)],
        mine,
        both,
        scratch=[total_scratch],
        work=work,
    )
    images, mine_left, pair_left, total_one = call(
        images_kernel,
        [single(8, height), single(8, height), single(8, height), single(8, packed)],
        mine,
        other,
        scaling,
        left_one,
        partial,
        factors,
        work=work,
    )
    left_two, values, wide_left = call(
        functools.partial(project_kernel, True),
        [single(8, height), single(4, packed), single(4, wide)],
        *reduced(images),
        both,
        mine_left,
        pair_left,
        total_one,
        scratch=[terms_scratch],
        work=work,
    )
    (update,) = call(
        update_kernel,
        [single(height, width)],
        *summed(values, wide_left),
        scaling,
        mine_left,
        left_two,
        total_one,
        out_specs=[hbm],
        scratch=[
            total_scratch,
            pltpu.VMEM((8, height), jnp.float32),
            pltpu.VMEM((CHUNKS, height, width // CHUNKS), jnp.float32),
            pltpu.SemaphoreType.DMA((CHUNKS,)),
        ],
        work=work,
    )
    return update


def solution(mesh):
    in_specs = (P("row", "col"), P(), P())
    out_specs = P("row", "col")

    return jax.shard_map(per_device, mesh=mesh, in_specs=in_specs, out_specs=out_specs, check_vma=False)
```

```python
import functools

import jax
import jax.numpy as jnp
from jax import lax
from jax.experimental import pallas as pl
from jax.experimental.pallas import tpu as pltpu
from jax.sharding import PartitionSpec as P

MODULUS_BITS = 13
MODULUS = (1 << MODULUS_BITS) - 1
LANES = 128
TAIL = 2 * LANES
CHUNKS = 5

epsilon = 1e-06
over_last = (((1,), (1,)), ((), ()))
over_inner = (((1,), (0,)), ((), ()))
over_first = (((0,), (0,)), ((), ()))


class Layout:
    def __init__(self, graph_rows, graph_cols):
        self.rows, self.cols = lax.axis_size("row"), lax.axis_size("col")
        self.nodes = (graph_rows, graph_cols)
        self.shards = (self.rows // graph_rows, self.cols // graph_cols)

    def exchange(self, value, target):
        pairs = []
        for r in range(self.rows):
            for c in range(self.cols):
                tr, tc = target(r, c)
                pairs.append((r * self.cols + c, tr * self.cols + tc))
        return lax.ppermute(value, ("row", "col"), pairs)

    def row_swap(self, value, bit):
        return self.exchange(value, lambda r, c: (r ^ 1 << bit, c))

    def col_swap(self, value, bit):
        return self.exchange(value, lambda r, c: (r, c ^ 1 << bit))

    def step(self, half, by):
        def target(r, c):
            if (r & 1) == half:
                return (r + by * self.shards[0]) % self.rows, c
            return r, (c + by * self.shards[1]) % self.cols

        return target

    def neighbours(self, value, half):
        if self.nodes == (2, 2):
            return self.exchange(value, self.step(half, 1))
        fours = value.reshape(-1, 2, 2, value.shape[1])
        after = self.exchange(fours[:, 1], self.step(half, -1))
        before = self.exchange(fours[:, 0], self.step(half, 1))
        return jnp.stack([after, before], 1).reshape(value.shape)

    def edges(self):
        row_index, col_index = lax.axis_index("row"), lax.axis_index("col")
        node = (row_index // self.shards[0], col_index // self.shards[1])
        found = []
        for half in range(2):
            along_col = (row_index & 1) ^ half
            for slot in range(2):
                owner = []
                for axis in range(2):
                    if self.nodes == (2, 2):
                        mine = slot
                    else:
                        mine = lax.rem(node[axis] + self.nodes[axis] - slot, self.nodes[axis])
                    owner.append(jnp.where(along_col == axis, mine, node[axis]))
                found.append((owner[0], owner[1], along_col))
        return found

    def first_column(self, width):
        return lax.rem(lax.axis_index("col"), self.shards[1]) * width


def stacked(values):
    high = values.astype(jnp.bfloat16).astype(jnp.float32)
    return jnp.concatenate([high, values - high], 0).astype(jnp.bfloat16)


def folded(product):
    half = product.shape[0] // 2
    return product[:half] + product[half:]


def dot(left, right, dims):
    return lax.dot_general(left, right, dims, preferred_element_type=jnp.float32)


def full_product(left, right, dims):
    high = right.astype(jnp.bfloat16)
    low = (right - high.astype(jnp.float32)).astype(jnp.bfloat16)
    terms = stacked(left)
    return folded(dot(terms, high, dims) + dot(terms, low, dims))


def remainder(value):
    value = (value & MODULUS) + (value >> MODULUS_BITS)
    value = (value & MODULUS) + (value >> MODULUS_BITS)
    return jnp.where(value >= MODULUS, value - MODULUS, value)


def row_values(scalars, width):
    rows = lax.broadcasted_iota(jnp.int32, (len(scalars), width), 0)
    values = jnp.full((len(scalars), width), scalars[0], jnp.int32)
    for k in range(1, len(scalars)):
        values = jnp.where(rows == k, scalars[k], values)
    return values


def first_kernel(
    layout, seeds_hbm, counts_hbm, replicas_hbm, keep_ref, send_ref, scaling_ref, replicas_ref, seeds_ref, counts_ref, sems
):
    size = replicas_ref.shape[1] // CHUNKS
    blocks = [pl.ds(k * size, size) for k in range(CHUNKS)]
    small = [
        pltpu.make_async_copy(seeds_hbm, seeds_ref, sems.at[CHUNKS]),
        pltpu.make_async_copy(counts_hbm, counts_ref, sems.at[CHUNKS + 1]),
    ]
    copies = [
        pltpu.make_async_copy(replicas_hbm.at[:, block], replicas_ref.at[:, block], sems.at[k])
        for k, block in enumerate(blocks)
    ]
    for copy in small + copies:
        copy.start()
    column = layout.first_column(replicas_ref.shape[1]) + lax.broadcasted_iota(
        jnp.int32, (8, replicas_ref.shape[1]), 1
    )
    square = remainder(column * column)
    edges = layout.edges()
    for copy in small:
        copy.wait()
    seeds = row_values([seeds_ref[r, c, a, k] for r, c, a in edges for k in range(2)], LANES)
    counts = row_values([counts_ref[r, c, a] for r, c, a in edges for _ in range(2)], LANES)
    scaling_ref[...] = -(counts.astype(jnp.float32) / 16.0)
    residue = remainder(square * (seeds[:, :1] + 1) + column * 17)
    factors = stacked(residue.astype(jnp.float32) * (2.0 / MODULUS) - 1.0)
    images = 0.0
    for k, block in enumerate(blocks):
        copies[k].wait()
        images = images + dot(factors[:, k * size : (k + 1) * size], replicas_ref[:, block], over_last)
    images = folded(images)
    keep_ref[...] = images[0:4]
    send_ref[...] = images[4:8]


def widen_kernel(values_ref, out_ref):
    out_ref[...] = values_ref[...].astype(jnp.float32)


def narrow_kernel(mine_ref, values_ref, out_ref):
    height = mine_ref.shape[0]
    out_ref[:height] = mine_ref[...]
    out_ref[height:] = values_ref[...].astype(jnp.bfloat16)


def upper(shape):
    return lax.broadcasted_iota(jnp.int32, shape, 0) < 4


def halves_added(values):
    return values + pltpu.roll(values, 4, 0)


def project_kernel(has_update, images_ref, neighbour_ref, both_ref, *refs):
    if has_update:
        mine_left_ref, pair_left_ref, right_ref, left_ref, packed_ref, wide_ref, terms_ref = refs
    else:
        left_ref, packed_ref, wide_ref, terms_ref = refs
    left = images_ref[...] - neighbour_ref[...]
    left_ref[...] = left
    height, width = left.shape[1], both_ref.shape[1]
    wide_ref[:, :height] = left[0:4]
    wide_ref[:, wide_ref.shape[1] // 2 : wide_ref.shape[1] // 2 + height] = left[4:8]
    high = left.astype(jnp.bfloat16).astype(jnp.float32)
    low = left - high
    terms_ref[:, :height] = jnp.where(upper(left.shape), high, pltpu.roll(low, 4, 0))
    terms_ref[:, height:] = jnp.where(upper(left.shape), pltpu.roll(high, 4, 0), low)
    projections = dot(terms_ref[...].astype(jnp.bfloat16), both_ref[...], over_inner)
    if has_update:
        cross = jnp.where(
            upper((8, 8)),
            full_product(left, mine_left_ref[...], over_last),
            full_product(left, pair_left_ref[...], over_last),
        )
        projections = projections + full_product(cross, right_ref[:, :width], over_inner)
    norm = jnp.sum(left * left, 1, keepdims=True)
    inner = jnp.sum(left * partners(left), 1, keepdims=True)
    packed_ref[:, :width] = halves_added(projections)[0:4]
    packed_ref[:, width : width + LANES] = halves_added(jnp.broadcast_to(norm, (8, LANES)))[0:4]
    packed_ref[:, width + LANES :] = halves_added(jnp.broadcast_to(inner, (8, LANES)))[0:4]


def is_even(shape):
    return lax.broadcasted_iota(jnp.int32, shape, 0) % 2 == 0


def partners(values):
    return jnp.where(is_even(values.shape), pltpu.roll(values, 7, 0), pltpu.roll(values, 1, 0))


def across(coefficient, width):
    return jnp.concatenate([coefficient] * -(-width // LANES), 1)[:, :width]


def coefficients(total_ref, width):
    norm = 0.5 * total_ref[:, width : width + LANES]
    inner = 0.5 * total_ref[:, width + LANES :]
    other = partners(norm)
    even = is_even(norm.shape)
    lead = lax.rsqrt(jnp.where(even, norm, other) + epsilon)
    correlation = inner * lead
    rest = jnp.where(even, other, norm) - correlation * correlation * (1.0 + epsilon * lead * lead)
    rest = lax.rsqrt(jnp.maximum(rest, 0.0) + epsilon)
    return lead, rest, -correlation * lead * rest


def rotated(raw, lead, rest, mixed):
    even = is_even(lead.shape)
    own, before = jnp.where(even, lead, rest), jnp.where(even, 0.0, mixed)
    width = raw.shape[1]
    return across(own, width) * raw + across(before, width) * pltpu.roll(raw, 1, 0)


def weighted(left, scaling, lead, rest, mixed):
    own = scaling * jnp.where(is_even(lead.shape), lead * lead + mixed * mixed, rest * rest)
    other = scaling * mixed * rest
    width = left.shape[1]
    return across(own, width) * left + across(other, width) * partners(left)


def own_kernel(mine_ref, both_ref, images_ref, factors_ref, total_ref):
    height, width = images_ref.shape[1], both_ref.shape[1]
    total_ref[0:4] = mine_ref[:, : width + TAIL]
    total_ref[4:8] = mine_ref[:, : width + TAIL]
    factors = rotated(total_ref[:, :width], *coefficients(total_ref, width))
    high = factors.astype(jnp.bfloat16).astype(jnp.float32)
    terms = jnp.where(upper(factors.shape), high, factors - high).astype(jnp.bfloat16)
    factors_ref[...] = factors
    images = halves_added(dot(terms, both_ref[...], over_last))
    images_ref[...] = jnp.where(
        upper((8, height)), images[:, :height], images[:, height : 2 * height]
    )


def images_kernel(
    mine_ref, other_ref, scaling_ref, left_ref, partial_ref, factors_ref,
    images_ref, mine_left_ref, pair_left_ref, total_ref,
):
    height, width = left_ref.shape[1], factors_ref.shape[1]
    first = width + TAIL
    second = first + (other_ref.shape[1] - first) // 2
    total_ref[0:4] = mine_ref[:, :first]
    total_ref[4:8] = other_ref[:, :first]
    cross = folded(dot(stacked(factors_ref[...]), stacked(total_ref[:, :width]), over_last))
    mine_left_ref[0:4] = left_ref[0:4]
    mine_left_ref[4:8] = other_ref[:, second : second + height]
    pair_left_ref[0:4] = left_ref[4:8]
    pair_left_ref[4:8] = other_ref[:, first : first + height]
    parts = coefficients(total_ref, width)
    scaling = scaling_ref[...]
    mine_left = weighted(mine_left_ref[...], scaling, *parts)
    pair_left = weighted(pair_left_ref[...], scaling, *parts)
    mine_left_ref[...] = mine_left
    pair_left_ref[...] = pair_left
    images_ref[...] = partial_ref[...] + jnp.where(
        upper((8, height)),
        full_product(cross, jnp.concatenate([mine_left] * 2, 0), over_inner),
        full_product(cross, jnp.concatenate([pair_left] * 2, 0), over_inner),
    )


def update_kernel(
    mine_ref, other_ref, scaling_ref, first_ref, left_ref, right_ref, out_ref, total_ref, second_ref, block_ref, sems
):
    height, width = left_ref.shape[1], out_ref.shape[1]
    packed = width + TAIL
    total_ref[0:4] = mine_ref[:, :packed]
    total_ref[4:8] = other_ref[:, :packed]
    start = packed + (other_ref.shape[1] - packed) // 2
    second_ref[0:4] = left_ref[0:4]
    second_ref[4:8] = other_ref[:, start : start + height]
    second = weighted(second_ref[...], scaling_ref[...], *coefficients(total_ref, width))
    lefts = jnp.concatenate([first_ref[...], second], 0)
    left_high = lefts.astype(jnp.bfloat16).astype(jnp.float32)
    left_terms = jnp.concatenate([left_high, lefts - left_high, left_high], 0).astype(jnp.bfloat16)
    size = block_ref.shape[2]
    copies = []
    for k in range(block_ref.shape[0]):
        columns = pl.ds(k * size, size)
        rights = jnp.concatenate([right_ref[:, columns], total_ref[:, columns]], 0)
        right_high = rights.astype(jnp.bfloat16).astype(jnp.float32)
        right_terms = jnp.concatenate([right_high, right_high, rights - right_high], 0)
        block_ref[k] = dot(left_terms, right_terms.astype(jnp.bfloat16), over_first)
        copies.append(pltpu.make_async_copy(block_ref.at[k], out_ref.at[:, columns], sems.at[k]))
        copies[-1].start()
    for copy in copies:
        copy.wait()


vmem = pl.BlockSpec(memory_space=pltpu.VMEM)
hbm = pl.BlockSpec(memory_space=pltpu.HBM)


def call(kernel, outs, *args, in_specs=None, out_specs=None, scratch=(), work=0):
    return pl.pallas_call(
        kernel,
        out_shape=outs,
        in_specs=in_specs or [vmem] * len(args),
        out_specs=out_specs or [vmem] * len(outs),
        scratch_shapes=list(scratch),
        compiler_params=pltpu.CompilerParams(vmem_limit_bytes=16 << 20),
        cost_estimate=pl.CostEstimate(flops=work, bytes_accessed=work, transcendentals=0),
    )(*args)


def single(*shape):
    return jax.ShapeDtypeStruct(shape, jnp.float32)


def per_device(replicas_hbm, factor_seeds, edge_counts):
    height, width = replicas_hbm.shape
    packed = width + TAIL
    wide = 2 * (-(-height // LANES) * LANES)
    layout = Layout(*factor_seeds.shape[:2])
    total_scratch = pltpu.VMEM((8, packed), jnp.float32)
    work = replicas_hbm.size

    def reduced(images):
        for bit in range(layout.shards[1].bit_length() - 1):
            images = images + layout.col_swap(images, bit)
        return images, layout.neighbours(images, 0)

    def summed(total, left):
        for bit in range(1, layout.shards[0].bit_length() - 1):
            total = total + layout.row_swap(total, bit)
        total = jnp.concatenate([total + layout.neighbours(total, 0), left], 1)
        return total, layout.row_swap(total, 0)

    keep, send, scaling, replicas = call(
        functools.partial(first_kernel, layout),
        [
            single(4, height),
            single(4, height),
            single(8, LANES),
            jax.ShapeDtypeStruct((height, width), replicas_hbm.dtype),
        ],
        *(
            pltpu.with_memory_space_constraint(array, pltpu.HBM)
            for array in (factor_seeds, edge_counts, replicas_hbm)
        ),
        in_specs=[hbm] * 3,
        scratch=[
            pltpu.SMEM(factor_seeds.shape, jnp.int32),
            pltpu.SMEM(edge_counts.shape, jnp.int32),
            pltpu.SemaphoreType.DMA((CHUNKS + 2,)),
        ],
        work=work,
    )
    taken = layout.row_swap(send, 0)
    images = jnp.concatenate([keep, taken], 0)
    (widened,) = call(widen_kernel, [single(height, width)], replicas, work=work)
    swapped = layout.row_swap(widened, 0)
    (both,) = call(
        narrow_kernel,
        [jax.ShapeDtypeStruct((2 * height, width), replicas_hbm.dtype)],
        replicas,
        swapped,
        work=work,
    )
    terms_scratch = pltpu.VMEM((8, 2 * height), jnp.float32)
    left_one, values, wide_left = call(
        functools.partial(project_kernel, False),
        [single(8, height), single(4, packed), single(4, wide)],
        *reduced(images),
        both,
        scratch=[terms_scratch],
        work=work,
    )
    mine, other = summed(values, wide_left)
    partial, factors = call(
        own_kernel,
        [single(8, height), single(8, width)],
        mine,
        both,
        scratch=[total_scratch],
        work=work,
    )
    images, mine_left, pair_left, total_one = call(
        images_kernel,
        [single(8, height), single(8, height), single(8, height), single(8, packed)],
        mine,
        other,
        scaling,
        left_one,
        partial,
        factors,
        work=work,
    )
    left_two, values, wide_left = call(
        functools.partial(project_kernel, True),
        [single(8, height), single(4, packed), single(4, wide)],
        *reduced(images),
        both,
        mine_left,
        pair_left,
        total_one,
        scratch=[terms_scratch],
        work=work,
    )
    (update,) = call(
        update_kernel,
        [single(height, width)],
        *summed(values, wide_left),
        scaling,
        mine_left,
        left_two,
        total_one,
        out_specs=[hbm],
        scratch=[
            total_scratch,
            pltpu.VMEM((8, height), jnp.float32),
            pltpu.VMEM((CHUNKS, height, width // CHUNKS), jnp.float32),
            pltpu.SemaphoreType.DMA((CHUNKS,)),
        ],
        work=work,
    )
    return update


def solution(mesh):
    in_specs = (P("row", "col"), P(), P())
    out_specs = P("row", "col")

    return jax.shard_map(per_device, mesh=mesh, in_specs=in_specs, out_specs=out_specs, check_vma=False)
```

```python
import functools

import jax
import jax.numpy as jnp
from jax import lax
from jax.experimental import pallas as pl
from jax.experimental.pallas import tpu as pltpu
from jax.sharding import PartitionSpec as P

MODULUS_BITS = 13
MODULUS = (1 << MODULUS_BITS) - 1
LANES = 128
TAIL = 2 * LANES
CHUNKS = 5
READS = 2

epsilon = 1e-06
over_last = (((1,), (1,)), ((), ()))
over_inner = (((1,), (0,)), ((), ()))
over_first = (((0,), (0,)), ((), ()))


class Layout:
    def __init__(self, graph_rows, graph_cols):
        self.rows, self.cols = lax.axis_size("row"), lax.axis_size("col")
        self.nodes = (graph_rows, graph_cols)
        self.shards = (self.rows // graph_rows, self.cols // graph_cols)

    def exchange(self, value, target):
        pairs = []
        for r in range(self.rows):
            for c in range(self.cols):
                tr, tc = target(r, c)
                pairs.append((r * self.cols + c, tr * self.cols + tc))
        return lax.ppermute(value, ("row", "col"), pairs)

    def row_swap(self, value, bit):
        return self.exchange(value, lambda r, c: (r ^ 1 << bit, c))

    def col_swap(self, value, bit):
        return self.exchange(value, lambda r, c: (r, c ^ 1 << bit))

    def step(self, half, by):
        def target(r, c):
            if (r & 1) == half:
                return (r + by * self.shards[0]) % self.rows, c
            return r, (c + by * self.shards[1]) % self.cols

        return target

    def neighbours(self, value, half):
        if self.nodes == (2, 2):
            return self.exchange(value, self.step(half, 1))
        fours = value.reshape(-1, 2, 2, value.shape[1])
        after = self.exchange(fours[:, 1], self.step(half, -1))
        before = self.exchange(fours[:, 0], self.step(half, 1))
        return jnp.stack([after, before], 1).reshape(value.shape)

    def edges(self):
        row_index, col_index = lax.axis_index("row"), lax.axis_index("col")
        node = (row_index // self.shards[0], col_index // self.shards[1])
        found = []
        for half in range(2):
            along_col = (row_index & 1) ^ half
            for slot in range(2):
                owner = []
                for axis in range(2):
                    if self.nodes == (2, 2):
                        mine = slot
                    else:
                        mine = lax.rem(node[axis] + self.nodes[axis] - slot, self.nodes[axis])
                    owner.append(jnp.where(along_col == axis, mine, node[axis]))
                found.append((owner[0], owner[1], along_col))
        return found

    def first_column(self, width):
        return lax.rem(lax.axis_index("col"), self.shards[1]) * width


def stacked(values):
    high = values.astype(jnp.bfloat16).astype(jnp.float32)
    return jnp.concatenate([high, values - high], 0).astype(jnp.bfloat16)


def folded(product):
    half = product.shape[0] // 2
    return product[:half] + product[half:]


def dot(left, right, dims):
    return lax.dot_general(left, right, dims, preferred_element_type=jnp.float32)


def full_product(left, right, dims):
    high = right.astype(jnp.bfloat16)
    low = (right - high.astype(jnp.float32)).astype(jnp.bfloat16)
    terms = stacked(left)
    return folded(dot(terms, high, dims) + dot(terms, low, dims))


def remainder(value):
    value = (value & MODULUS) + (value >> MODULUS_BITS)
    value = (value & MODULUS) + (value >> MODULUS_BITS)
    return jnp.where(value >= MODULUS, value - MODULUS, value)


def row_values(scalars, width):
    rows = lax.broadcasted_iota(jnp.int32, (len(scalars), width), 0)
    values = jnp.full((len(scalars), width), scalars[0], jnp.int32)
    for k in range(1, len(scalars)):
        values = jnp.where(rows == k, scalars[k], values)
    return values


def first_kernel(
    layout, seeds_hbm, counts_hbm, replicas_hbm, keep_ref, send_ref, scaling_ref, replicas_ref,
    seeds_ref, counts_ref, terms_ref, sum_ref, sems
):
    size = replicas_ref.shape[1] // READS

    def read(k):
        block = pl.ds(pl.multiple_of(k * size, LANES), size)
        return pltpu.make_async_copy(replicas_hbm.at[:, block], replicas_ref.at[:, block], sems.at[k]), block

    small = [
        pltpu.make_async_copy(seeds_hbm, seeds_ref, sems.at[READS]),
        pltpu.make_async_copy(counts_hbm, counts_ref, sems.at[READS + 1]),
    ]
    for copy in small + [read(k)[0] for k in range(READS)]:
        copy.start()
    column = layout.first_column(replicas_ref.shape[1]) + lax.broadcasted_iota(
        jnp.int32, (8, replicas_ref.shape[1]), 1
    )
    square = remainder(column * column)
    edges = layout.edges()
    for copy in small:
        copy.wait()
    seeds = row_values([seeds_ref[r, c, a, k] for r, c, a in edges for k in range(2)], LANES)
    counts = row_values([counts_ref[r, c, a] for r, c, a in edges for _ in range(2)], LANES)
    scaling_ref[...] = -(counts.astype(jnp.float32) / 16.0)
    residue = remainder(square * (seeds[:, :1] + 1) + column * 17)
    terms_ref[...] = stacked(residue.astype(jnp.float32) * (2.0 / MODULUS) - 1.0)
    sum_ref[...] = jnp.zeros_like(sum_ref)

    @pl.loop(0, READS)
    def _(k):
        copy, block = read(k)
        copy.wait()
        sum_ref[...] += dot(terms_ref[:, block], replicas_ref[:, block], over_last)

    images = folded(sum_ref[...])
    keep_ref[...] = images[0:4]
    send_ref[...] = images[4:8]


def widen_kernel(values_ref, out_ref):
    out_ref[...] = values_ref[...].astype(jnp.float32)


def narrow_kernel(mine_ref, values_ref, out_ref):
    height = mine_ref.shape[0]
    out_ref[:height] = mine_ref[...]
    out_ref[height:] = values_ref[...].astype(jnp.bfloat16)


def upper(shape):
    return lax.broadcasted_iota(jnp.int32, shape, 0) < 4


def halves_added(values):
    return values + pltpu.roll(values, 4, 0)


def project_kernel(has_update, images_ref, neighbour_ref, both_ref, *refs):
    if has_update:
        mine_left_ref, pair_left_ref, right_ref, left_ref, packed_ref, wide_ref, terms_ref = refs
    else:
        left_ref, packed_ref, wide_ref, terms_ref = refs
    left = images_ref[...] - neighbour_ref[...]
    left_ref[...] = left
    height, width = left.shape[1], both_ref.shape[1]
    wide_ref[:, :height] = left[0:4]
    wide_ref[:, wide_ref.shape[1] // 2 : wide_ref.shape[1] // 2 + height] = left[4:8]
    high = left.astype(jnp.bfloat16).astype(jnp.float32)
    low = left - high
    terms_ref[:, :height] = jnp.where(upper(left.shape), high, pltpu.roll(low, 4, 0))
    terms_ref[:, height:] = jnp.where(upper(left.shape), pltpu.roll(high, 4, 0), low)
    projections = dot(terms_ref[...].astype(jnp.bfloat16), both_ref[...], over_inner)
    if has_update:
        cross = jnp.where(
            upper((8, 8)),
            full_product(left, mine_left_ref[...], over_last),
            full_product(left, pair_left_ref[...], over_last),
        )
        projections = projections + full_product(cross, right_ref[:, :width], over_inner)
    norm = jnp.sum(left * left, 1, keepdims=True)
    inner = jnp.sum(left * partners(left), 1, keepdims=True)
    packed_ref[:, :width] = halves_added(projections)[0:4]
    packed_ref[:, width : width + LANES] = halves_added(jnp.broadcast_to(norm, (8, LANES)))[0:4]
    packed_ref[:, width + LANES :] = halves_added(jnp.broadcast_to(inner, (8, LANES)))[0:4]


def is_even(shape):
    return lax.broadcasted_iota(jnp.int32, shape, 0) % 2 == 0


def partners(values):
    return jnp.where(is_even(values.shape), pltpu.roll(values, 7, 0), pltpu.roll(values, 1, 0))


def across(coefficient, width):
    return jnp.concatenate([coefficient] * -(-width // LANES), 1)[:, :width]


def coefficients(total_ref, width):
    norm = 0.5 * total_ref[:, width : width + LANES]
    inner = 0.5 * total_ref[:, width + LANES :]
    other = partners(norm)
    even = is_even(norm.shape)
    lead = lax.rsqrt(jnp.where(even, norm, other) + epsilon)
    correlation = inner * lead
    rest = jnp.where(even, other, norm) - correlation * correlation * (1.0 + epsilon * lead * lead)
    rest = lax.rsqrt(jnp.maximum(rest, 0.0) + epsilon)
    return lead, rest, -correlation * lead * rest


def rotated(raw, lead, rest, mixed):
    even = is_even(lead.shape)
    own, before = jnp.where(even, lead, rest), jnp.where(even, 0.0, mixed)
    width = raw.shape[1]
    return across(own, width) * raw + across(before, width) * pltpu.roll(raw, 1, 0)


def weighted(left, scaling, lead, rest, mixed):
    own = scaling * jnp.where(is_even(lead.shape), lead * lead + mixed * mixed, rest * rest)
    other = scaling * mixed * rest
    width = left.shape[1]
    return across(own, width) * left + across(other, width) * partners(left)


def own_kernel(mine_ref, both_ref, images_ref, factors_ref, total_ref):
    height, width = images_ref.shape[1], both_ref.shape[1]
    total_ref[0:4] = mine_ref[:, : width + TAIL]
    total_ref[4:8] = mine_ref[:, : width + TAIL]
    factors = rotated(total_ref[:, :width], *coefficients(total_ref, width))
    high = factors.astype(jnp.bfloat16).astype(jnp.float32)
    terms = jnp.where(upper(factors.shape), high, factors - high).astype(jnp.bfloat16)
    factors_ref[...] = factors
    images = halves_added(dot(terms, both_ref[...], over_last))
    images_ref[...] = jnp.where(
        upper((8, height)), images[:, :height], images[:, height : 2 * height]
    )


def images_kernel(
    mine_ref, other_ref, scaling_ref, left_ref, partial_ref, factors_ref,
    images_ref, mine_left_ref, pair_left_ref, total_ref,
):
    height, width = left_ref.shape[1], factors_ref.shape[1]
    first = width + TAIL
    second = first + (other_ref.shape[1] - first) // 2
    total_ref[0:4] = mine_ref[:, :first]
    total_ref[4:8] = other_ref[:, :first]
    cross = folded(dot(stacked(factors_ref[...]), stacked(total_ref[:, :width]), over_last))
    mine_left_ref[0:4] = left_ref[0:4]
    mine_left_ref[4:8] = other_ref[:, second : second + height]
    pair_left_ref[0:4] = left_ref[4:8]
    pair_left_ref[4:8] = other_ref[:, first : first + height]
    parts = coefficients(total_ref, width)
    scaling = scaling_ref[...]
    mine_left = weighted(mine_left_ref[...], scaling, *parts)
    pair_left = weighted(pair_left_ref[...], scaling, *parts)
    mine_left_ref[...] = mine_left
    pair_left_ref[...] = pair_left
    images_ref[...] = partial_ref[...] + jnp.where(
        upper((8, height)),
        full_product(cross, jnp.concatenate([mine_left] * 2, 0), over_inner),
        full_product(cross, jnp.concatenate([pair_left] * 2, 0), over_inner),
    )


def update_kernel(
    mine_ref, other_ref, scaling_ref, first_ref, left_ref, right_ref, out_ref, total_ref, second_ref, block_ref, sems
):
    height, width = left_ref.shape[1], out_ref.shape[1]
    packed = width + TAIL
    total_ref[0:4] = mine_ref[:, :packed]
    total_ref[4:8] = other_ref[:, :packed]
    start = packed + (other_ref.shape[1] - packed) // 2
    second_ref[0:4] = left_ref[0:4]
    second_ref[4:8] = other_ref[:, start : start + height]
    second = weighted(second_ref[...], scaling_ref[...], *coefficients(total_ref, width))
    lefts = jnp.concatenate([first_ref[...], second], 0)
    left_high = lefts.astype(jnp.bfloat16).astype(jnp.float32)
    left_terms = jnp.concatenate([left_high, lefts - left_high, left_high], 0).astype(jnp.bfloat16)
    size = block_ref.shape[2]
    copies = []
    for k in range(block_ref.shape[0]):
        columns = pl.ds(k * size, size)
        rights = jnp.concatenate([right_ref[:, columns], total_ref[:, columns]], 0)
        right_high = rights.astype(jnp.bfloat16).astype(jnp.float32)
        right_terms = jnp.concatenate([right_high, right_high, rights - right_high], 0)
        block_ref[k] = dot(left_terms, right_terms.astype(jnp.bfloat16), over_first)
        copies.append(pltpu.make_async_copy(block_ref.at[k], out_ref.at[:, columns], sems.at[k]))
        copies[-1].start()
    for copy in copies:
        copy.wait()


vmem = pl.BlockSpec(memory_space=pltpu.VMEM)
hbm = pl.BlockSpec(memory_space=pltpu.HBM)


def call(kernel, outs, *args, in_specs=None, out_specs=None, scratch=(), work=0):
    return pl.pallas_call(
        kernel,
        out_shape=outs,
        in_specs=in_specs or [vmem] * len(args),
        out_specs=out_specs or [vmem] * len(outs),
        scratch_shapes=list(scratch),
        compiler_params=pltpu.CompilerParams(vmem_limit_bytes=16 << 20),
        cost_estimate=pl.CostEstimate(flops=work, bytes_accessed=work, transcendentals=0),
    )(*args)


def single(*shape):
    return jax.ShapeDtypeStruct(shape, jnp.float32)


def per_device(replicas_hbm, factor_seeds, edge_counts):
    height, width = replicas_hbm.shape
    packed = width + TAIL
    wide = 2 * (-(-height // LANES) * LANES)
    layout = Layout(*factor_seeds.shape[:2])
    total_scratch = pltpu.VMEM((8, packed), jnp.float32)
    work = replicas_hbm.size

    def reduced(images):
        for bit in range(layout.shards[1].bit_length() - 1):
            images = images + layout.col_swap(images, bit)
        return images, layout.neighbours(images, 0)

    def summed(total, left):
        for bit in range(1, layout.shards[0].bit_length() - 1):
            total = total + layout.row_swap(total, bit)
        total = jnp.concatenate([total + layout.neighbours(total, 0), left], 1)
        return total, layout.row_swap(total, 0)

    keep, send, scaling, replicas = call(
        functools.partial(first_kernel, layout),
        [
            single(4, height),
            single(4, height),
            single(8, LANES),
            jax.ShapeDtypeStruct((height, width), replicas_hbm.dtype),
        ],
        *(
            pltpu.with_memory_space_constraint(array, pltpu.HBM)
            for array in (factor_seeds, edge_counts, replicas_hbm)
        ),
        in_specs=[hbm] * 3,
        scratch=[
            pltpu.SMEM(factor_seeds.shape, jnp.int32),
            pltpu.SMEM(edge_counts.shape, jnp.int32),
            pltpu.VMEM((16, width), jnp.bfloat16),
            pltpu.VMEM((16, height), jnp.float32),
            pltpu.SemaphoreType.DMA((READS + 2,)),
        ],
        work=work,
    )
    taken = layout.row_swap(send, 0)
    images = jnp.concatenate([keep, taken], 0)
    (widened,) = call(widen_kernel, [single(height, width)], replicas, work=work)
    swapped = layout.row_swap(widened, 0)
    (both,) = call(
        narrow_kernel,
        [jax.ShapeDtypeStruct((2 * height, width), replicas_hbm.dtype)],
        replicas,
        swapped,
        work=work,
    )
    terms_scratch = pltpu.VMEM((8, 2 * height), jnp.float32)
    left_one, values, wide_left = call(
        functools.partial(project_kernel, False),
        [single(8, height), single(4, packed), single(4, wide)],
        *reduced(images),
        both,
        scratch=[terms_scratch],
        work=work,
    )
    mine, other = summed(values, wide_left)
    partial, factors = call(
        own_kernel,
        [single(8, height), single(8, width)],
        mine,
        both,
        scratch=[total_scratch],
        work=work,
    )
    images, mine_left, pair_left, total_one = call(
        images_kernel,
        [single(8, height), single(8, height), single(8, height), single(8, packed)],
        mine,
        other,
        scaling,
        left_one,
        partial,
        factors,
        work=work,
    )
    left_two, values, wide_left = call(
        functools.partial(project_kernel, True),
        [single(8, height), single(4, packed), single(4, wide)],
        *reduced(images),
        both,
        mine_left,
        pair_left,
        total_one,
        scratch=[terms_scratch],
        work=work,
    )
    (update,) = call(
        update_kernel,
        [single(height, width)],
        *summed(values, wide_left),
        scaling,
        mine_left,
        left_two,
        total_one,
        out_specs=[hbm],
        scratch=[
            total_scratch,
            pltpu.VMEM((8, height), jnp.float32),
            pltpu.VMEM((CHUNKS, height, width // CHUNKS), jnp.float32),
            pltpu.SemaphoreType.DMA((CHUNKS,)),
        ],
        work=work,
    )
    return update


def solution(mesh):
    in_specs = (P("row", "col"), P(), P())
    out_specs = P("row", "col")

    return jax.shard_map(per_device, mesh=mesh, in_specs=in_specs, out_specs=out_specs, check_vma=False)
```

```python
import functools

import jax
import jax.numpy as jnp
from jax import lax
from jax.experimental import pallas as pl
from jax.experimental.pallas import tpu as pltpu
from jax.sharding import PartitionSpec as P

MODULUS_BITS = 13
MODULUS = (1 << MODULUS_BITS) - 1
LANES = 128
TAIL = 2 * LANES
CHUNKS = 5
READS = 2

epsilon = 1e-06
over_last = (((1,), (1,)), ((), ()))
over_inner = (((1,), (0,)), ((), ()))
over_first = (((0,), (0,)), ((), ()))


class Layout:
    def __init__(self, graph_rows, graph_cols):
        self.rows, self.cols = lax.axis_size("row"), lax.axis_size("col")
        self.nodes = (graph_rows, graph_cols)
        self.shards = (self.rows // graph_rows, self.cols // graph_cols)

    def exchange(self, value, target):
        pairs = []
        for r in range(self.rows):
            for c in range(self.cols):
                tr, tc = target(r, c)
                pairs.append((r * self.cols + c, tr * self.cols + tc))
        return lax.ppermute(value, ("row", "col"), pairs)

    def row_flip(self, bit):
        return lambda r, c: (r ^ 1 << bit, c)

    def col_flip(self, bit):
        return lambda r, c: (r, c ^ 1 << bit)

    def row_swap(self, value, bit):
        return self.exchange(value, self.row_flip(bit))

    def step(self, half, by):
        def target(r, c):
            if (r & 1) == half:
                return (r + by * self.shards[0]) % self.rows, c
            return r, (c + by * self.shards[1]) % self.cols

        return target

    def neighbours(self, value, flip=None):
        def target(by):
            step = self.step(0, by)
            return step if flip is None else lambda r, c: flip(*step(r, c))

        if self.nodes == (2, 2):
            return self.exchange(value, target(1))
        fours = value.reshape(-1, 2, 2, value.shape[1])
        after = self.exchange(fours[:, 1], target(-1))
        before = self.exchange(fours[:, 0], target(1))
        return jnp.stack([after, before], 1).reshape(value.shape)

    def gathered(self, value, flips):
        for flip in flips[:-1]:
            value = value + self.exchange(value, flip)
        own, other = [value], []
        for flip in flips[-1:]:
            own.append(self.exchange(value, flip))
        other.append(self.neighbours(value))
        for flip in flips[-1:]:
            other.append(self.neighbours(value, flip))
        return own, other

    def edges(self):
        row_index, col_index = lax.axis_index("row"), lax.axis_index("col")
        node = (row_index // self.shards[0], col_index // self.shards[1])
        found = []
        for half in range(2):
            along_col = (row_index & 1) ^ half
            for slot in range(2):
                owner = []
                for axis in range(2):
                    if self.nodes == (2, 2):
                        mine = slot
                    else:
                        mine = lax.rem(node[axis] + self.nodes[axis] - slot, self.nodes[axis])
                    owner.append(jnp.where(along_col == axis, mine, node[axis]))
                found.append((owner[0], owner[1], along_col))
        return found

    def first_column(self, width):
        return lax.rem(lax.axis_index("col"), self.shards[1]) * width


def stacked(values):
    high = values.astype(jnp.bfloat16).astype(jnp.float32)
    return jnp.concatenate([high, values - high], 0).astype(jnp.bfloat16)


def folded(product):
    half = product.shape[0] // 2
    return product[:half] + product[half:]


def dot(left, right, dims):
    return lax.dot_general(left, right, dims, preferred_element_type=jnp.float32)


def full_product(left, right, dims):
    high = right.astype(jnp.bfloat16)
    low = (right - high.astype(jnp.float32)).astype(jnp.bfloat16)
    terms = stacked(left)
    return folded(dot(terms, high, dims) + dot(terms, low, dims))


def remainder(value):
    value = (value & MODULUS) + (value >> MODULUS_BITS)
    value = (value & MODULUS) + (value >> MODULUS_BITS)
    return jnp.where(value >= MODULUS, value - MODULUS, value)


def row_values(scalars, width):
    rows = lax.broadcasted_iota(jnp.int32, (len(scalars), width), 0)
    values = jnp.full((len(scalars), width), scalars[0], jnp.int32)
    for k in range(1, len(scalars)):
        values = jnp.where(rows == k, scalars[k], values)
    return values


def first_kernel(
    layout, seeds_hbm, counts_hbm, replicas_hbm, keep_ref, send_ref, scaling_ref, replicas_ref,
    seeds_ref, counts_ref, terms_ref, sum_ref, sems
):
    size = replicas_ref.shape[1] // READS

    def read(k):
        block = pl.ds(pl.multiple_of(k * size, LANES), size)
        return pltpu.make_async_copy(replicas_hbm.at[:, block], replicas_ref.at[:, block], sems.at[k]), block

    small = [
        pltpu.make_async_copy(seeds_hbm, seeds_ref, sems.at[READS]),
        pltpu.make_async_copy(counts_hbm, counts_ref, sems.at[READS + 1]),
    ]
    for copy in small + [read(k)[0] for k in range(READS)]:
        copy.start()
    column = layout.first_column(replicas_ref.shape[1]) + lax.broadcasted_iota(
        jnp.int32, (8, replicas_ref.shape[1]), 1
    )
    square = remainder(column * column)
    edges = layout.edges()
    for copy in small:
        copy.wait()
    seeds = row_values([seeds_ref[r, c, a, k] for r, c, a in edges for k in range(2)], LANES)
    counts = row_values([counts_ref[r, c, a] for r, c, a in edges for _ in range(2)], LANES)
    scaling_ref[...] = -(counts.astype(jnp.float32) / 16.0)
    residue = remainder(square * (seeds[:, :1] + 1) + column * 17)
    terms_ref[...] = stacked(residue.astype(jnp.float32) * (2.0 / MODULUS) - 1.0)
    sum_ref[...] = jnp.zeros_like(sum_ref)

    @pl.loop(0, READS)
    def _(k):
        copy, block = read(k)
        copy.wait()
        sum_ref[...] += dot(terms_ref[:, block], replicas_ref[:, block], over_last)

    images = folded(sum_ref[...])
    keep_ref[...] = images[0:4]
    send_ref[...] = images[4:8]


def widen_kernel(values_ref, out_ref):
    out_ref[...] = values_ref[...].astype(jnp.float32)


def narrow_kernel(mine_ref, values_ref, out_ref):
    height = mine_ref.shape[0]
    out_ref[:height] = mine_ref[...]
    out_ref[height:] = values_ref[...].astype(jnp.bfloat16)


def upper(shape):
    return lax.broadcasted_iota(jnp.int32, shape, 0) < 4


def halves_added(values):
    return values + pltpu.roll(values, 4, 0)


def project_kernel(has_update, count, *refs):
    own_refs, other_refs, both_ref, refs = refs[:count], refs[count : 2 * count], refs[2 * count], refs[2 * count + 1 :]
    if has_update:
        mine_left_ref, pair_left_ref, right_ref, left_ref, packed_ref, wide_ref, terms_ref = refs
    else:
        left_ref, packed_ref, wide_ref, terms_ref = refs
    left = sum(ref[...] for ref in own_refs) - sum(ref[...] for ref in other_refs)
    left_ref[...] = left
    height, width = left.shape[1], both_ref.shape[1]
    wide_ref[:, :height] = left[0:4]
    wide_ref[:, wide_ref.shape[1] // 2 : wide_ref.shape[1] // 2 + height] = left[4:8]
    high = left.astype(jnp.bfloat16).astype(jnp.float32)
    low = left - high
    terms_ref[:, :height] = jnp.where(upper(left.shape), high, pltpu.roll(low, 4, 0))
    terms_ref[:, height:] = jnp.where(upper(left.shape), pltpu.roll(high, 4, 0), low)
    projections = dot(terms_ref[...].astype(jnp.bfloat16), both_ref[...], over_inner)
    if has_update:
        cross = jnp.where(
            upper((8, 8)),
            full_product(left, mine_left_ref[...], over_last),
            full_product(left, pair_left_ref[...], over_last),
        )
        projections = projections + full_product(cross, right_ref[:, :width], over_inner)
    norm = jnp.sum(left * left, 1, keepdims=True)
    inner = jnp.sum(left * partners(left), 1, keepdims=True)
    packed_ref[:, :width] = halves_added(projections)[0:4]
    packed_ref[:, width : width + LANES] = halves_added(jnp.broadcast_to(norm, (8, LANES)))[0:4]
    packed_ref[:, width + LANES :] = halves_added(jnp.broadcast_to(inner, (8, LANES)))[0:4]


def is_even(shape):
    return lax.broadcasted_iota(jnp.int32, shape, 0) % 2 == 0


def partners(values):
    return jnp.where(is_even(values.shape), pltpu.roll(values, 7, 0), pltpu.roll(values, 1, 0))


def across(coefficient, width):
    return jnp.concatenate([coefficient] * -(-width // LANES), 1)[:, :width]


def coefficients(total_ref, width):
    norm = 0.5 * total_ref[:, width : width + LANES]
    inner = 0.5 * total_ref[:, width + LANES :]
    other = partners(norm)
    even = is_even(norm.shape)
    lead = lax.rsqrt(jnp.where(even, norm, other) + epsilon)
    correlation = inner * lead
    rest = jnp.where(even, other, norm) - correlation * correlation * (1.0 + epsilon * lead * lead)
    rest = lax.rsqrt(jnp.maximum(rest, 0.0) + epsilon)
    return lead, rest, -correlation * lead * rest


def rotated(raw, lead, rest, mixed):
    even = is_even(lead.shape)
    own, before = jnp.where(even, lead, rest), jnp.where(even, 0.0, mixed)
    width = raw.shape[1]
    return across(own, width) * raw + across(before, width) * pltpu.roll(raw, 1, 0)


def weighted(left, scaling, lead, rest, mixed):
    own = scaling * jnp.where(is_even(lead.shape), lead * lead + mixed * mixed, rest * rest)
    other = scaling * mixed * rest
    width = left.shape[1]
    return across(own, width) * left + across(other, width) * partners(left)


def own_kernel(mine_ref, both_ref, images_ref, factors_ref, total_ref):
    height, width = images_ref.shape[1], both_ref.shape[1]
    total_ref[0:4] = mine_ref[:, : width + TAIL]
    total_ref[4:8] = mine_ref[:, : width + TAIL]
    factors = rotated(total_ref[:, :width], *coefficients(total_ref, width))
    high = factors.astype(jnp.bfloat16).astype(jnp.float32)
    terms = jnp.where(upper(factors.shape), high, factors - high).astype(jnp.bfloat16)
    factors_ref[...] = factors
    images = halves_added(dot(terms, both_ref[...], over_last))
    images_ref[...] = jnp.where(
        upper((8, height)), images[:, :height], images[:, height : 2 * height]
    )


def images_kernel(
    mine_ref, other_ref, scaling_ref, left_ref, partial_ref, factors_ref,
    images_ref, mine_left_ref, pair_left_ref, total_ref,
):
    height, width = left_ref.shape[1], factors_ref.shape[1]
    first = width + TAIL
    second = first + (other_ref.shape[1] - first) // 2
    total_ref[0:4] = mine_ref[:, :first]
    total_ref[4:8] = other_ref[:, :first]
    cross = folded(dot(stacked(factors_ref[...]), stacked(total_ref[:, :width]), over_last))
    mine_left_ref[0:4] = left_ref[0:4]
    mine_left_ref[4:8] = other_ref[:, second : second + height]
    pair_left_ref[0:4] = left_ref[4:8]
    pair_left_ref[4:8] = other_ref[:, first : first + height]
    parts = coefficients(total_ref, width)
    scaling = scaling_ref[...]
    mine_left = weighted(mine_left_ref[...], scaling, *parts)
    pair_left = weighted(pair_left_ref[...], scaling, *parts)
    mine_left_ref[...] = mine_left
    pair_left_ref[...] = pair_left
    images_ref[...] = partial_ref[...] + jnp.where(
        upper((8, height)),
        full_product(cross, jnp.concatenate([mine_left] * 2, 0), over_inner),
        full_product(cross, jnp.concatenate([pair_left] * 2, 0), over_inner),
    )


def update_kernel(
    mine_ref, other_ref, scaling_ref, first_ref, left_ref, right_ref, out_ref, total_ref, second_ref, block_ref, sems
):
    height, width = left_ref.shape[1], out_ref.shape[1]
    packed = width + TAIL
    total_ref[0:4] = mine_ref[:, :packed]
    total_ref[4:8] = other_ref[:, :packed]
    start = packed + (other_ref.shape[1] - packed) // 2
    second_ref[0:4] = left_ref[0:4]
    second_ref[4:8] = other_ref[:, start : start + height]
    second = weighted(second_ref[...], scaling_ref[...], *coefficients(total_ref, width))
    lefts = jnp.concatenate([first_ref[...], second], 0)
    left_high = lefts.astype(jnp.bfloat16).astype(jnp.float32)
    left_terms = jnp.concatenate([left_high, lefts - left_high, left_high], 0).astype(jnp.bfloat16)
    size = block_ref.shape[2]
    copies = []
    for k in range(block_ref.shape[0]):
        columns = pl.ds(k * size, size)
        rights = jnp.concatenate([right_ref[:, columns], total_ref[:, columns]], 0)
        right_high = rights.astype(jnp.bfloat16).astype(jnp.float32)
        right_terms = jnp.concatenate([right_high, right_high, rights - right_high], 0)
        block_ref[k] = dot(left_terms, right_terms.astype(jnp.bfloat16), over_first)
        copies.append(pltpu.make_async_copy(block_ref.at[k], out_ref.at[:, columns], sems.at[k]))
        copies[-1].start()
    for copy in copies:
        copy.wait()


vmem = pl.BlockSpec(memory_space=pltpu.VMEM)
hbm = pl.BlockSpec(memory_space=pltpu.HBM)


def call(kernel, outs, *args, in_specs=None, out_specs=None, scratch=(), work=0):
    return pl.pallas_call(
        kernel,
        out_shape=outs,
        in_specs=in_specs or [vmem] * len(args),
        out_specs=out_specs or [vmem] * len(outs),
        scratch_shapes=list(scratch),
        compiler_params=pltpu.CompilerParams(vmem_limit_bytes=16 << 20),
        cost_estimate=pl.CostEstimate(flops=work, bytes_accessed=work, transcendentals=0),
    )(*args)


def single(*shape):
    return jax.ShapeDtypeStruct(shape, jnp.float32)


def per_device(replicas_hbm, factor_seeds, edge_counts):
    height, width = replicas_hbm.shape
    packed = width + TAIL
    wide = 2 * (-(-height // LANES) * LANES)
    layout = Layout(*factor_seeds.shape[:2])
    total_scratch = pltpu.VMEM((8, packed), jnp.float32)
    work = replicas_hbm.size

    col_flips = [layout.col_flip(bit) for bit in range(layout.shards[1].bit_length() - 1)]
    row_flips = [layout.row_flip(bit) for bit in range(1, layout.shards[0].bit_length() - 1)]

    def reduced(images):
        own, other = layout.gathered(images, col_flips)
        return own + other

    def summed(values, left):
        own, other = layout.gathered(values, row_flips)
        total = jnp.concatenate([sum(own) + sum(other), left], 1)
        return total, layout.row_swap(total, 0)

    keep, send, scaling, replicas = call(
        functools.partial(first_kernel, layout),
        [
            single(4, height),
            single(4, height),
            single(8, LANES),
            jax.ShapeDtypeStruct((height, width), replicas_hbm.dtype),
        ],
        *(
            pltpu.with_memory_space_constraint(array, pltpu.HBM)
            for array in (factor_seeds, edge_counts, replicas_hbm)
        ),
        in_specs=[hbm] * 3,
        scratch=[
            pltpu.SMEM(factor_seeds.shape, jnp.int32),
            pltpu.SMEM(edge_counts.shape, jnp.int32),
            pltpu.VMEM((16, width), jnp.bfloat16),
            pltpu.VMEM((16, height), jnp.float32),
            pltpu.SemaphoreType.DMA((READS + 2,)),
        ],
        work=work,
    )
    taken = layout.row_swap(send, 0)
    images = jnp.concatenate([keep, taken], 0)
    (widened,) = call(widen_kernel, [single(height, width)], replicas, work=work)
    swapped = layout.row_swap(widened, 0)
    (both,) = call(
        narrow_kernel,
        [jax.ShapeDtypeStruct((2 * height, width), replicas_hbm.dtype)],
        replicas,
        swapped,
        work=work,
    )
    terms_scratch = pltpu.VMEM((8, 2 * height), jnp.float32)
    count = min(len(col_flips), 1) + 1
    left_one, values, wide_left = call(
        functools.partial(project_kernel, False, count),
        [single(8, height), single(4, packed), single(4, wide)],
        *reduced(images),
        both,
        scratch=[terms_scratch],
        work=work,
    )
    mine, other = summed(values, wide_left)
    partial, factors = call(
        own_kernel,
        [single(8, height), single(8, width)],
        mine,
        both,
        scratch=[total_scratch],
        work=work,
    )
    images, mine_left, pair_left, total_one = call(
        images_kernel,
        [single(8, height), single(8, height), single(8, height), single(8, packed)],
        mine,
        other,
        scaling,
        left_one,
        partial,
        factors,
        work=work,
    )
    left_two, values, wide_left = call(
        functools.partial(project_kernel, True, count),
        [single(8, height), single(4, packed), single(4, wide)],
        *reduced(images),
        both,
        mine_left,
        pair_left,
        total_one,
        scratch=[terms_scratch],
        work=work,
    )
    (update,) = call(
        update_kernel,
        [single(height, width)],
        *summed(values, wide_left),
        scaling,
        mine_left,
        left_two,
        total_one,
        out_specs=[hbm],
        scratch=[
            total_scratch,
            pltpu.VMEM((8, height), jnp.float32),
            pltpu.VMEM((CHUNKS, height, width // CHUNKS), jnp.float32),
            pltpu.SemaphoreType.DMA((CHUNKS,)),
        ],
        work=work,
    )
    return update


def solution(mesh):
    in_specs = (P("row", "col"), P(), P())
    out_specs = P("row", "col")

    return jax.shard_map(per_device, mesh=mesh, in_specs=in_specs, out_specs=out_specs, check_vma=False)
```

```python
import functools

import jax
import jax.numpy as jnp
from jax import lax
from jax.experimental import pallas as pl
from jax.experimental.pallas import tpu as pltpu
from jax.sharding import PartitionSpec as P

MODULUS_BITS = 13
MODULUS = (1 << MODULUS_BITS) - 1
LANES = 128
TAIL = 2 * LANES
PARTS = (1, 2, 2, 2, 3)
READS = 2

epsilon = 1e-06
over_last = (((1,), (1,)), ((), ()))
over_inner = (((1,), (0,)), ((), ()))
over_first = (((0,), (0,)), ((), ()))


class Layout:
    def __init__(self, graph_rows, graph_cols):
        self.rows, self.cols = lax.axis_size("row"), lax.axis_size("col")
        self.nodes = (graph_rows, graph_cols)
        self.shards = (self.rows // graph_rows, self.cols // graph_cols)

    def exchange(self, value, target):
        pairs = []
        for r in range(self.rows):
            for c in range(self.cols):
                tr, tc = target(r, c)
                pairs.append((r * self.cols + c, tr * self.cols + tc))
        return lax.ppermute(value, ("row", "col"), pairs)

    def row_flip(self, bit):
        return lambda r, c: (r ^ 1 << bit, c)

    def col_flip(self, bit):
        return lambda r, c: (r, c ^ 1 << bit)

    def row_swap(self, value, bit):
        return self.exchange(value, self.row_flip(bit))

    def step(self, half, by):
        def target(r, c):
            if (r & 1) == half:
                return (r + by * self.shards[0]) % self.rows, c
            return r, (c + by * self.shards[1]) % self.cols

        return target

    def neighbours(self, value, flip=None):
        def target(by):
            step = self.step(0, by)
            return step if flip is None else lambda r, c: flip(*step(r, c))

        if self.nodes == (2, 2):
            return self.exchange(value, target(1))
        fours = value.reshape(-1, 2, 2, value.shape[1])
        after = self.exchange(fours[:, 1], target(-1))
        before = self.exchange(fours[:, 0], target(1))
        return jnp.stack([after, before], 1).reshape(value.shape)

    def gathered(self, value, flips):
        for flip in flips[:-1]:
            value = value + self.exchange(value, flip)
        own, other = [value], []
        for flip in flips[-1:]:
            own.append(self.exchange(value, flip))
        other.append(self.neighbours(value))
        for flip in flips[-1:]:
            other.append(self.neighbours(value, flip))
        return own, other

    def edges(self):
        row_index, col_index = lax.axis_index("row"), lax.axis_index("col")
        node = (row_index // self.shards[0], col_index // self.shards[1])
        found = []
        for half in range(2):
            along_col = (row_index & 1) ^ half
            for slot in range(2):
                owner = []
                for axis in range(2):
                    if self.nodes == (2, 2):
                        mine = slot
                    else:
                        mine = lax.rem(node[axis] + self.nodes[axis] - slot, self.nodes[axis])
                    owner.append(jnp.where(along_col == axis, mine, node[axis]))
                found.append((owner[0], owner[1], along_col))
        return found

    def first_column(self, width):
        return lax.rem(lax.axis_index("col"), self.shards[1]) * width


def stacked(values):
    high = values.astype(jnp.bfloat16).astype(jnp.float32)
    return jnp.concatenate([high, values - high], 0).astype(jnp.bfloat16)


def folded(product):
    half = product.shape[0] // 2
    return product[:half] + product[half:]


def dot(left, right, dims):
    return lax.dot_general(left, right, dims, preferred_element_type=jnp.float32)


def full_product(left, right, dims):
    high = right.astype(jnp.bfloat16)
    low = (right - high.astype(jnp.float32)).astype(jnp.bfloat16)
    terms = stacked(left)
    return folded(dot(terms, high, dims) + dot(terms, low, dims))


def remainder(value):
    value = (value & MODULUS) + (value >> MODULUS_BITS)
    value = (value & MODULUS) + (value >> MODULUS_BITS)
    return jnp.where(value >= MODULUS, value - MODULUS, value)


def row_values(scalars, width):
    rows = lax.broadcasted_iota(jnp.int32, (len(scalars), width), 0)
    values = jnp.full((len(scalars), width), scalars[0], jnp.int32)
    for k in range(1, len(scalars)):
        values = jnp.where(rows == k, scalars[k], values)
    return values


def first_kernel(
    layout, seeds_hbm, counts_hbm, replicas_hbm, keep_ref, send_ref, scaling_ref, replicas_ref,
    seeds_ref, counts_ref, terms_ref, sum_ref, sems
):
    size = replicas_ref.shape[1] // READS

    def read(k):
        block = pl.ds(pl.multiple_of(k * size, LANES), size)
        return pltpu.make_async_copy(replicas_hbm.at[:, block], replicas_ref.at[:, block], sems.at[k]), block

    small = [
        pltpu.make_async_copy(seeds_hbm, seeds_ref, sems.at[READS]),
        pltpu.make_async_copy(counts_hbm, counts_ref, sems.at[READS + 1]),
    ]
    for copy in small + [read(k)[0] for k in range(READS)]:
        copy.start()
    column = layout.first_column(replicas_ref.shape[1]) + lax.broadcasted_iota(
        jnp.int32, (8, replicas_ref.shape[1]), 1
    )
    square = remainder(column * column)
    edges = layout.edges()
    for copy in small:
        copy.wait()
    seeds = row_values([seeds_ref[r, c, a, k] for r, c, a in edges for k in range(2)], LANES)
    counts = row_values([counts_ref[r, c, a] for r, c, a in edges for _ in range(2)], LANES)
    scaling_ref[...] = -(counts.astype(jnp.float32) / 16.0)
    residue = remainder(square * (seeds[:, :1] + 1) + column * 17)
    terms_ref[...] = stacked(residue.astype(jnp.float32) * (2.0 / MODULUS) - 1.0)
    sum_ref[...] = jnp.zeros_like(sum_ref)

    @pl.loop(0, READS)
    def _(k):
        copy, block = read(k)
        copy.wait()
        sum_ref[...] += dot(terms_ref[:, block], replicas_ref[:, block], over_last)

    images = folded(sum_ref[...])
    keep_ref[...] = images[0:4]
    send_ref[...] = images[4:8]


def widen_kernel(values_ref, out_ref):
    out_ref[...] = values_ref[...].astype(jnp.float32)


def narrow_kernel(mine_ref, values_ref, out_ref):
    height = mine_ref.shape[0]
    out_ref[:height] = mine_ref[...]
    out_ref[height:] = values_ref[...].astype(jnp.bfloat16)


def upper(shape):
    return lax.broadcasted_iota(jnp.int32, shape, 0) < 4


def halves_added(values):
    return values + pltpu.roll(values, 4, 0)


def project_kernel(has_update, count, *refs):
    own_refs, other_refs, both_ref, refs = refs[:count], refs[count : 2 * count], refs[2 * count], refs[2 * count + 1 :]
    if has_update:
        mine_left_ref, pair_left_ref, right_ref, left_ref, packed_ref, wide_ref, terms_ref = refs
    else:
        left_ref, packed_ref, wide_ref, terms_ref = refs
    left = sum(ref[...] for ref in own_refs) - sum(ref[...] for ref in other_refs)
    left_ref[...] = left
    height, width = left.shape[1], both_ref.shape[1]
    wide_ref[:, :height] = left[0:4]
    wide_ref[:, wide_ref.shape[1] // 2 : wide_ref.shape[1] // 2 + height] = left[4:8]
    high = left.astype(jnp.bfloat16).astype(jnp.float32)
    low = left - high
    terms_ref[:, :height] = jnp.where(upper(left.shape), high, pltpu.roll(low, 4, 0))
    terms_ref[:, height:] = jnp.where(upper(left.shape), pltpu.roll(high, 4, 0), low)
    projections = dot(terms_ref[...].astype(jnp.bfloat16), both_ref[...], over_inner)
    if has_update:
        cross = jnp.where(
            upper((8, 8)),
            full_product(left, mine_left_ref[...], over_last),
            full_product(left, pair_left_ref[...], over_last),
        )
        projections = projections + full_product(cross, right_ref[:, :width], over_inner)
    norm = jnp.sum(left * left, 1, keepdims=True)
    inner = jnp.sum(left * partners(left), 1, keepdims=True)
    packed_ref[:, :width] = halves_added(projections)[0:4]
    packed_ref[:, width : width + LANES] = halves_added(jnp.broadcast_to(norm, (8, LANES)))[0:4]
    packed_ref[:, width + LANES :] = halves_added(jnp.broadcast_to(inner, (8, LANES)))[0:4]


def is_even(shape):
    return lax.broadcasted_iota(jnp.int32, shape, 0) % 2 == 0


def partners(values):
    return jnp.where(is_even(values.shape), pltpu.roll(values, 7, 0), pltpu.roll(values, 1, 0))


def across(coefficient, width):
    return jnp.concatenate([coefficient] * -(-width // LANES), 1)[:, :width]


def coefficients(total_ref, width):
    norm = 0.5 * total_ref[:, width : width + LANES]
    inner = 0.5 * total_ref[:, width + LANES :]
    other = partners(norm)
    even = is_even(norm.shape)
    lead = lax.rsqrt(jnp.where(even, norm, other) + epsilon)
    correlation = inner * lead
    rest = jnp.where(even, other, norm) - correlation * correlation * (1.0 + epsilon * lead * lead)
    rest = lax.rsqrt(jnp.maximum(rest, 0.0) + epsilon)
    return lead, rest, -correlation * lead * rest


def rotated(raw, lead, rest, mixed):
    even = is_even(lead.shape)
    own, before = jnp.where(even, lead, rest), jnp.where(even, 0.0, mixed)
    width = raw.shape[1]
    return across(own, width) * raw + across(before, width) * pltpu.roll(raw, 1, 0)


def weighted(left, scaling, lead, rest, mixed):
    own = scaling * jnp.where(is_even(lead.shape), lead * lead + mixed * mixed, rest * rest)
    other = scaling * mixed * rest
    width = left.shape[1]
    return across(own, width) * left + across(other, width) * partners(left)


def own_kernel(mine_ref, both_ref, images_ref, factors_ref, total_ref):
    height, width = images_ref.shape[1], both_ref.shape[1]
    total_ref[0:4] = mine_ref[:, : width + TAIL]
    total_ref[4:8] = mine_ref[:, : width + TAIL]
    factors = rotated(total_ref[:, :width], *coefficients(total_ref, width))
    high = factors.astype(jnp.bfloat16).astype(jnp.float32)
    terms = jnp.where(upper(factors.shape), high, factors - high).astype(jnp.bfloat16)
    factors_ref[...] = factors
    images = halves_added(dot(terms, both_ref[...], over_last))
    images_ref[...] = jnp.where(
        upper((8, height)), images[:, :height], images[:, height : 2 * height]
    )


def images_kernel(
    mine_ref, other_ref, scaling_ref, left_ref, partial_ref, factors_ref,
    images_ref, mine_left_ref, pair_left_ref, total_ref,
):
    height, width = left_ref.shape[1], factors_ref.shape[1]
    first = width + TAIL
    second = first + (other_ref.shape[1] - first) // 2
    total_ref[0:4] = mine_ref[:, :first]
    total_ref[4:8] = other_ref[:, :first]
    cross = folded(dot(stacked(factors_ref[...]), stacked(total_ref[:, :width]), over_last))
    mine_left_ref[0:4] = left_ref[0:4]
    mine_left_ref[4:8] = other_ref[:, second : second + height]
    pair_left_ref[0:4] = left_ref[4:8]
    pair_left_ref[4:8] = other_ref[:, first : first + height]
    parts = coefficients(total_ref, width)
    scaling = scaling_ref[...]
    mine_left = weighted(mine_left_ref[...], scaling, *parts)
    pair_left = weighted(pair_left_ref[...], scaling, *parts)
    mine_left_ref[...] = mine_left
    pair_left_ref[...] = pair_left
    images_ref[...] = partial_ref[...] + jnp.where(
        upper((8, height)),
        full_product(cross, jnp.concatenate([mine_left] * 2, 0), over_inner),
        full_product(cross, jnp.concatenate([pair_left] * 2, 0), over_inner),
    )


def update_kernel(
    mine_ref, other_ref, scaling_ref, first_ref, left_ref, right_ref, out_ref, total_ref, second_ref, block_ref, sems
):
    height, width = left_ref.shape[1], out_ref.shape[1]
    packed = width + TAIL
    total_ref[0:4] = mine_ref[:, :packed]
    total_ref[4:8] = other_ref[:, :packed]
    start = packed + (other_ref.shape[1] - packed) // 2
    second_ref[0:4] = left_ref[0:4]
    second_ref[4:8] = other_ref[:, start : start + height]
    second = weighted(second_ref[...], scaling_ref[...], *coefficients(total_ref, width))
    lefts = jnp.concatenate([first_ref[...], second], 0)
    left_high = lefts.astype(jnp.bfloat16).astype(jnp.float32)
    left_terms = jnp.concatenate([left_high, lefts - left_high, left_high], 0).astype(jnp.bfloat16)
    unit = width // sum(PARTS)
    copies = []
    for k, part in enumerate(PARTS):
        columns = pl.ds(sum(PARTS[:k]) * unit, part * unit)
        rights = jnp.concatenate([right_ref[:, columns], total_ref[:, columns]], 0)
        right_high = rights.astype(jnp.bfloat16).astype(jnp.float32)
        right_terms = jnp.concatenate([right_high, right_high, rights - right_high], 0)
        block_ref[:, columns] = dot(left_terms, right_terms.astype(jnp.bfloat16), over_first)
        copies.append(pltpu.make_async_copy(block_ref.at[:, columns], out_ref.at[:, columns], sems.at[k]))
        copies[-1].start()
    for copy in copies:
        copy.wait()


vmem = pl.BlockSpec(memory_space=pltpu.VMEM)
hbm = pl.BlockSpec(memory_space=pltpu.HBM)


def call(kernel, outs, *args, in_specs=None, out_specs=None, scratch=(), work=0):
    return pl.pallas_call(
        kernel,
        out_shape=outs,
        in_specs=in_specs or [vmem] * len(args),
        out_specs=out_specs or [vmem] * len(outs),
        scratch_shapes=list(scratch),
        compiler_params=pltpu.CompilerParams(vmem_limit_bytes=16 << 20),
        cost_estimate=pl.CostEstimate(flops=work, bytes_accessed=work, transcendentals=0),
    )(*args)


def single(*shape):
    return jax.ShapeDtypeStruct(shape, jnp.float32)


def per_device(replicas_hbm, factor_seeds, edge_counts):
    height, width = replicas_hbm.shape
    packed = width + TAIL
    wide = 2 * (-(-height // LANES) * LANES)
    layout = Layout(*factor_seeds.shape[:2])
    total_scratch = pltpu.VMEM((8, packed), jnp.float32)
    work = replicas_hbm.size

    col_flips = [layout.col_flip(bit) for bit in range(layout.shards[1].bit_length() - 1)]
    row_flips = [layout.row_flip(bit) for bit in range(1, layout.shards[0].bit_length() - 1)]

    def reduced(images):
        own, other = layout.gathered(images, col_flips)
        return own + other

    def summed(values, left):
        own, other = layout.gathered(values, row_flips)
        total = jnp.concatenate([sum(own) + sum(other), left], 1)
        return total, layout.row_swap(total, 0)

    keep, send, scaling, replicas = call(
        functools.partial(first_kernel, layout),
        [
            single(4, height),
            single(4, height),
            single(8, LANES),
            jax.ShapeDtypeStruct((height, width), replicas_hbm.dtype),
        ],
        *(
            pltpu.with_memory_space_constraint(array, pltpu.HBM)
            for array in (factor_seeds, edge_counts, replicas_hbm)
        ),
        in_specs=[hbm] * 3,
        scratch=[
            pltpu.SMEM(factor_seeds.shape, jnp.int32),
            pltpu.SMEM(edge_counts.shape, jnp.int32),
            pltpu.VMEM((16, width), jnp.bfloat16),
            pltpu.VMEM((16, height), jnp.float32),
            pltpu.SemaphoreType.DMA((READS + 2,)),
        ],
        work=work,
    )
    taken = layout.row_swap(send, 0)
    images = jnp.concatenate([keep, taken], 0)
    (widened,) = call(widen_kernel, [single(height, width)], replicas, work=work)
    swapped = layout.row_swap(widened, 0)
    (both,) = call(
        narrow_kernel,
        [jax.ShapeDtypeStruct((2 * height, width), replicas_hbm.dtype)],
        replicas,
        swapped,
        work=work,
    )
    terms_scratch = pltpu.VMEM((8, 2 * height), jnp.float32)
    count = min(len(col_flips), 1) + 1
    left_one, values, wide_left = call(
        functools.partial(project_kernel, False, count),
        [single(8, height), single(4, packed), single(4, wide)],
        *reduced(images),
        both,
        scratch=[terms_scratch],
        work=work,
    )
    mine, other = summed(values, wide_left)
    partial, factors = call(
        own_kernel,
        [single(8, height), single(8, width)],
        mine,
        both,
        scratch=[total_scratch],
        work=work,
    )
    images, mine_left, pair_left, total_one = call(
        images_kernel,
        [single(8, height), single(8, height), single(8, height), single(8, packed)],
        mine,
        other,
        scaling,
        left_one,
        partial,
        factors,
        work=work,
    )
    left_two, values, wide_left = call(
        functools.partial(project_kernel, True, count),
        [single(8, height), single(4, packed), single(4, wide)],
        *reduced(images),
        both,
        mine_left,
        pair_left,
        total_one,
        scratch=[terms_scratch],
        work=work,
    )
    (update,) = call(
        update_kernel,
        [single(height, width)],
        *summed(values, wide_left),
        scaling,
        mine_left,
        left_two,
        total_one,
        out_specs=[hbm],
        scratch=[
            total_scratch,
            pltpu.VMEM((8, height), jnp.float32),
            pltpu.VMEM((height, width), jnp.float32),
            pltpu.SemaphoreType.DMA((len(PARTS),)),
        ],
        work=work,
    )
    return update


def solution(mesh):
    in_specs = (P("row", "col"), P(), P())
    out_specs = P("row", "col")

    return jax.shard_map(per_device, mesh=mesh, in_specs=in_specs, out_specs=out_specs, check_vma=False)
```
